512 devices in a mesh: row: 4 (over y), col: 16 (over z), dep: 8 (over x, core).
Axes of the slice: x: 4, y: 4, z: 16, core: 2. Of those that a mesh axis runs over, the one named last changes fastest.
Arguments:
- matrix: float32 [16384, 16384], P('row', ('col', 'dep')), may hold values from -6 to 6
- vectors: float32 [64, 16384], P(None, ('row', 'col')), may hold values from -0.09375 to 0.09375
Outputs:
- reduced: float32 [16384, 16384], P('row', ('col', 'dep'))
The draws below stay inside these ranges and needn't reach their ends.
All inputs are finite; a program needn't handle non-finite values.
Results may differ from the reference program's by a relative error of at most 0.0001.
Values sent between devices are 32-bit elements; how exact they have to be, the bound alone decides.
No kernel may reach another device: no remote copies, remote signals or barrier semaphores. Data moves between devices by JAX's collectives and lax.ppermute only.
A program may use at most 64 MiB of HBM per device.

```python
import jax
import jax.numpy as jnp
from jax import lax

N = 16384
B = 64


def levels(rng, shape, shards, least, largest):
    factor_of = 1.0
    for axis_at, parts in shards:
        draws = jax.random.uniform(jax.random.fold_in(jax.random.fold_in(rng, 6), axis_at), (parts,), jnp.float32, least / len(shards), largest / len(shards))
        factor_of = factor_of * jnp.repeat(jnp.exp(draws), shape[axis_at] // parts).reshape((-1,) + (1,) * (len(shape) - 1 - axis_at))
    return factor_of


def centred(own_key, extent, scale, limit, pieces=(), kind=jnp.bfloat16):
    loudness = levels(own_key, extent, pieces, -0.22, 0.18) if pieces else 1.0
    values = jax.random.normal(own_key, extent, jnp.float32) * scale * loudness
    return jnp.minimum(jnp.maximum(values, -limit), limit).astype(kind)


def setup_inputs(seed: int = 0) -> dict:
    splits = jax.random.split(jax.random.key(seed), 3)
    return {
        "matrix": centred(splits[0], (N, N), 1.0, 6.0, ((0, 4), (1, 128)), jnp.float32),
        "vectors": centred(splits[1], (B, N), (N // 4) ** -0.5, 0.09375, ((1, 64),), jnp.float32),
    }


highest = lax.Precision.HIGHEST


def contract(left, right, dims):
    return lax.dot_general(left, right, (dims, ((), ())), precision=highest)


def mask_vectors(values, first_row):
    panel_width, row_count = values.shape
    positions = first_row + lax.iota(jnp.int32, row_count)[None, :]
    reflector = lax.iota(jnp.int32, panel_width)[:, None]
    filler = jnp.where(positions == reflector + 1, 1.0, 0.0).astype(values.dtype)
    return jnp.where(positions > reflector + 1, values, filler)


def make_factor(gram):
    size_b = gram.shape[0]
    half_diag = 0.5 * jnp.diagonal(gram)
    scaled = jnp.triu(gram, 1) / half_diag[:, None]
    identity = jnp.eye(size_b, dtype=gram.dtype)
    inverse = identity - scaled
    powered = scaled
    for level in range((size_b - 1).bit_length() - 1):
        powered = jnp.dot(powered, powered, precision=highest)
        inverse = jnp.dot(inverse, identity + powered, precision=highest)
    return inverse / half_diag[None, :]


def reference(matrix, vectors):
    reflectors = mask_vectors(vectors, 0)
    gram = contract(reflectors, reflectors, ((1,), (1,)))
    factor = make_factor(gram)
    products = contract(reflectors, matrix, ((1,), (1,)))
    update = contract(factor, products, ((0,), (0,)))
    right_done = matrix - contract(update, reflectors, ((0,), (0,)))
    left_terms = contract(reflectors, right_done, ((1,), (0,)))
    scaled_terms = contract(factor, left_terms, ((0,), (0,)))
    return right_done - contract(reflectors, scaled_terms, ((0,), (0,)))
```

```python
import jax
import jax.numpy as jnp
from jax import lax
from jax.experimental import pallas as pl
from jax.experimental.pallas import tpu as pltpu
from jax.sharding import Mesh
from jax.sharding import PartitionSpec as P

AXES = ("row", "zh", "zl", "x", "core")
COLUMNS = ("zh", "zl", "x", "core")
PLANE = ("zl", "x")
LANES = 128
WIDTH = 64

highest = lax.Precision.HIGHEST
NN = ((1,), (0,))
NT = ((1,), (1,))
TN = ((0,), (0,))


def exact(left, right, dims):
    return lax.dot_general(
        left, right, (dims, ((), ())), precision=highest, preferred_element_type=jnp.float32
    )


def split(array):
    high = array.astype(jnp.bfloat16)
    return high, (array - high.astype(jnp.float32)).astype(jnp.bfloat16)


def three_pass(left, right, dims):
    def dot(a, b):
        return lax.dot_general(a, b, (dims, ((), ())), preferred_element_type=jnp.float32)

    return dot(left[0], right[0]) + (dot(left[0], right[1]) + dot(left[1], right[0]))


def swapped(array, axes):
    return lax.all_to_all(array, axes, 0, 0, tiled=True)


def shared(array, axes):
    return swapped(jnp.broadcast_to(array, (lax.axis_size(axes), *array.shape)), axes)


def mask_vectors(values, first_row):
    panel_width, row_count = values.shape
    positions = first_row + lax.iota(jnp.int32, row_count)[None, :]
    reflector = lax.iota(jnp.int32, panel_width)[:, None]
    filler = jnp.where(positions == reflector + 1, 1.0, 0.0).astype(values.dtype)
    return jnp.where(positions > reflector + 1, values, filler)


def column_routes():
    turn = {0: 2, 1: 1, 2: 0, 3: 3}
    pairs = []
    for y in range(4):
        for z in range(16):
            for x in range(4):
                for core in range(2):
                    to_x, to_z = z % 4, y * 4 + z // 4
                    to_y = (y + turn[(x - to_x) % 4]) % 4
                    here = ((y * 16 + z) * 4 + x) * 2 + core
                    pairs.append((here, ((to_y * 16 + to_z) * 4 + to_x) * 2 + core))
    return pairs


def value_kernel(columns_ref, matrix_ref, out_ref):
    left = split(columns_ref[...])
    for k in range(8):
        right = split(matrix_ref[k * LANES : (k + 1) * LANES, :])
        out_ref[k] = three_pass(left, right, NT)


def partial_value(columns, matrix):
    return pl.pallas_call(
        value_kernel,
        grid=(4,),
        in_specs=[
            pl.BlockSpec((WIDTH, LANES), lambda i: (0, 0)),
            pl.BlockSpec((8 * LANES, LANES), lambda i: (i, 0)),
        ],
        out_specs=pl.BlockSpec((8, WIDTH, LANES), lambda i: (i, 0, 0)),
        out_shape=jax.ShapeDtypeStruct((32, WIDTH, LANES), jnp.float32),
        name="value",
    )(columns, matrix)


def reflector_block(joined_ref, step, k):
    start = pl.multiple_of(WIDTH + step * 16 + (k % 2) * 8, 8)
    return joined_ref[:, k // 2, :, pl.ds(start, 8), :].reshape(WIDTH, LANES)


def value_block(joined_ref, step, k):
    return joined_ref[step // 2, (step % 2) * 2 + k // 4, k % 4, :WIDTH, :]


def terms_kernel(joined_ref, matrix_ref, out_ref):
    step = pl.program_id(0)

    @pl.when(step == 0)
    def _():
        out_ref[...] = jnp.zeros_like(out_ref)

    plain = jnp.zeros((WIDTH, LANES), jnp.float32)
    inner = jnp.zeros((WIDTH, LANES), jnp.float32)
    for k in range(8):
        rows = reflector_block(joined_ref, step, k)
        left = split(rows)
        plain += three_pass(left, split(matrix_ref[k * LANES : (k + 1) * LANES, :]), NN)
        other = jnp.concatenate([value_block(joined_ref, step, k), rows], axis=0)
        inner += exact(rows, other, NT)
    out_ref[:, :LANES] += plain
    out_ref[:, LANES:] += inner


def left_parts(joined, matrix):
    return pl.pallas_call(
        terms_kernel,
        grid=(4,),
        in_specs=[
            pl.BlockSpec(joined.shape, lambda i: (0, 0, 0, 0, 0)),
            pl.BlockSpec((8 * LANES, LANES), lambda i: (i, 0)),
        ],
        out_specs=pl.BlockSpec((WIDTH, 2 * LANES), lambda i: (0, 0)),
        out_shape=jax.ShapeDtypeStruct((WIDTH, 2 * LANES), jnp.float32),
        name="terms",
    )(joined, matrix)


def make_factor(gram):
    size_b = gram.shape[0]
    down = lax.broadcasted_iota(jnp.int32, (size_b, size_b), 0)
    across = lax.broadcasted_iota(jnp.int32, (size_b, size_b), 1)
    identity = jnp.where(down == across, 1.0, 0.0)
    half = 0.5 * jnp.where(down == across, gram, 0.0)
    half_down = jnp.sum(half, axis=1, keepdims=True)
    half_across = jnp.sum(half, axis=0, keepdims=True)
    scaled = jnp.where(across > down, gram, 0.0) / half_down
    inverse = identity - scaled
    powered = scaled
    for level in range((size_b - 1).bit_length() - 1):
        powered = exact(powered, powered, NN)
        inverse = exact(inverse, identity + powered, NN)
    return inverse / half_across


def last_kernel(parts_ref, columns_ref, joined_ref, matrix_ref, out_ref, right_ref):
    step = pl.program_id(0)

    @pl.when(step == 0)
    def _():
        total = (parts_ref[0] + parts_ref[1]) + (parts_ref[2] + parts_ref[3])
        factor = make_factor(total[:, LANES + WIDTH :])
        right = exact(factor, columns_ref[...], NN)
        left = total[:, :LANES] - exact(total[:, LANES : LANES + WIDTH], right, NN)
        right_ref[:WIDTH, :] = right
        right_ref[WIDTH:, :] = exact(factor, left, TN)

    right = split(right_ref[...])
    for k in range(8):
        left = jnp.concatenate(
            [value_block(joined_ref, step, k), reflector_block(joined_ref, step, k)], axis=0
        )
        change = three_pass(split(left), right, TN)
        span = slice(k * LANES, (k + 1) * LANES)
        out_ref[span, :] = matrix_ref[span, :] - change


def last_step(parts, columns, joined, matrix):
    return pl.pallas_call(
        last_kernel,
        grid=(4,),
        in_specs=[
            pl.BlockSpec(parts.shape, lambda i: (0, 0, 0)),
            pl.BlockSpec((WIDTH, LANES), lambda i: (0, 0)),
            pl.BlockSpec(joined.shape, lambda i: (0, 0, 0, 0, 0)),
            pl.BlockSpec((8 * LANES, LANES), lambda i: (i, 0)),
        ],
        out_specs=pl.BlockSpec((8 * LANES, LANES), lambda i: (i, 0)),
        out_shape=jax.ShapeDtypeStruct(matrix.shape, jnp.float32),
        scratch_shapes=[pltpu.VMEM((2 * WIDTH, LANES), jnp.float32)],
        name="last",
    )(parts, columns, joined, matrix)


def on_device(matrix, vectors):
    width, piece = vectors.shape
    core, x = lax.axis_index("core"), lax.axis_index("x")
    masked = mask_vectors(vectors, lax.axis_index(("row", "zh", "zl")) * piece)
    half = lax.dynamic_slice_in_dim(masked, core * LANES, LANES, 1)
    columns = lax.ppermute(half, AXES, column_routes())
    lines = lax.dynamic_slice_in_dim(masked, (core * 4 + x) * 8, 8, 0)
    lines = lines.reshape(8, 2, LANES).swapaxes(0, 1).reshape(16, LANES)

    values = partial_value(columns, matrix)
    values = swapped(values.reshape(2, 16, WIDTH, LANES), "core").sum(axis=0)
    values = swapped(values, PLANE).sum(axis=0)
    far = shared(jnp.concatenate([values, lines], axis=0), "zh")
    summed = far[:, :WIDTH].sum(axis=0)
    own = jnp.concatenate([summed, far[:, WIDTH:].reshape(WIDTH, LANES)], axis=0)
    joined = shared(shared(own, PLANE), "core").reshape(2, 4, 4, 2 * WIDTH, LANES)

    parts = shared(left_parts(joined, matrix), "row")
    return last_step(parts, columns, joined, matrix)


def solution(mesh):
    torus = Mesh(mesh.devices.reshape(4, 4, 4, 4, 2), AXES)
    placed = (P("row", COLUMNS), P(None, ("row", "zh", "zl")))
    return jax.shard_map(
        on_device, mesh=torus, in_specs=placed, out_specs=P("row", COLUMNS), check_vma=False
    )
```

```python
import jax
import jax.numpy as jnp
from jax import lax
from jax.experimental import pallas as pl
from jax.experimental.pallas import tpu as pltpu
from jax.sharding import Mesh
from jax.sharding import PartitionSpec as P

AXES = ("row", "zh", "zl", "x", "core")
COLUMNS = ("zh", "zl", "x", "core")
PLANE = ("zl", "x")
LANES = 128
WIDTH = 64
ROOM = pltpu.CompilerParams(vmem_limit_bytes=16 * 1024 * 1024)

highest = lax.Precision.HIGHEST
NN = ((1,), (0,))
NT = ((1,), (1,))
TN = ((0,), (0,))


def exact(left, right, dims):
    return lax.dot_general(
        left, right, (dims, ((), ())), precision=highest, preferred_element_type=jnp.float32
    )


def split(array):
    high = array.astype(jnp.bfloat16)
    return high, (array - high.astype(jnp.float32)).astype(jnp.bfloat16)


def dot(left, right, dims):
    return lax.dot_general(left, right, (dims, ((), ())), preferred_element_type=jnp.float32)


def swapped(array, axes):
    return lax.all_to_all(array, axes, 0, 0, tiled=True)


def shared(array, axes):
    return swapped(jnp.broadcast_to(array, (lax.axis_size(axes), *array.shape)), axes)


def mask_vectors(values, first_row):
    panel_width, row_count = values.shape
    positions = first_row + lax.iota(jnp.int32, row_count)[None, :]
    reflector = lax.iota(jnp.int32, panel_width)[:, None]
    filler = jnp.where(positions == reflector + 1, 1.0, 0.0).astype(values.dtype)
    return jnp.where(positions > reflector + 1, values, filler)


def column_routes():
    turn = {0: 2, 1: 1, 2: 0, 3: 3}
    pairs = []
    for y in range(4):
        for z in range(16):
            for x in range(4):
                for core in range(2):
                    to_x, to_z = z % 4, y * 4 + z // 4
                    to_y = (y + turn[(x - to_x) % 4]) % 4
                    here = ((y * 16 + z) * 4 + x) * 2 + core
                    pairs.append((here, ((to_y * 16 + to_z) * 4 + to_x) * 2 + core))
    return pairs


def doubled(array):
    blank = jnp.zeros_like(array)
    return jnp.concatenate(
        [jnp.concatenate([array, blank], axis=1), jnp.concatenate([blank, array], axis=1)], axis=0
    )


def local(array):
    return pltpu.with_memory_space_constraint(array, pltpu.VMEM)


def in_vmem(count):
    return [pl.BlockSpec(memory_space=pltpu.VMEM)] * count


def value_kernel(columns_ref, matrix_ref, out_ref):
    high, low = split(doubled(columns_ref[...].T))
    right = jnp.concatenate([high, low], axis=1)
    for unit in range(16):
        first = matrix_ref[2 * unit * LANES : (2 * unit + 1) * LANES, :]
        second = matrix_ref[(2 * unit + 1) * LANES : (2 * unit + 2) * LANES, :]
        high, low = split(jnp.concatenate([first, second], axis=1))
        both = dot(high, right, NN) + dot(low, right, NN)
        total = both[:, :LANES] + both[:, LANES:]
        out_ref[2 * unit : 2 * unit + 2] = total.reshape(2, WIDTH, LANES)


def partial_value(columns, matrix):
    return pl.pallas_call(
        value_kernel,
        in_specs=in_vmem(2),
        out_specs=in_vmem(1)[0],
        out_shape=pltpu.VMEM((32, WIDTH, LANES), jnp.float32),
        compiler_params=ROOM,
        name="value",
    )(columns, matrix)


def reflector_block(joined_ref, unit, half):
    zh, zl = divmod(unit, 4)
    start = WIDTH + zh * 16 + half * 8
    return joined_ref[:, zl, :, start : start + 8, :].reshape(WIDTH, LANES)


def value_unit(joined_ref, unit):
    piece = 2 * unit
    core, zl, x = piece // 16, piece // 4 % 4, piece % 4
    return joined_ref[core, zl, x : x + 2, :WIDTH, :].reshape(2 * WIDTH, LANES)


def in_three(array):
    high, low = split(array)
    rest = array - high.astype(jnp.float32) - low.astype(jnp.float32)
    return jnp.concatenate([high, low, rest.astype(jnp.bfloat16)], axis=0)


def terms_kernel(joined_ref, matrix_ref, out_ref):
    plain = jnp.zeros((2 * WIDTH, 2 * LANES), jnp.float32)
    cross = jnp.zeros((4 * WIDTH, 2 * LANES), jnp.float32)
    gram = jnp.zeros((3 * WIDTH, 3 * WIDTH), jnp.float32)
    for unit in range(16):
        rows = [reflector_block(joined_ref, unit, half) for half in range(2)]
        rows = in_three(jnp.concatenate(rows, axis=1))
        span = slice(2 * unit * LANES, 2 * (unit + 1) * LANES)
        right = jnp.concatenate(split(matrix_ref[span, :]), axis=1)
        plain += dot(rows[: 2 * WIDTH], right, NN)
        right = jnp.concatenate(split(value_unit(joined_ref, unit)), axis=1)
        both = [rows[: 2 * WIDTH, :LANES], rows[: 2 * WIDTH, LANES:]]
        cross += dot(jnp.concatenate(both, axis=0), right, NN)
        gram += dot(rows, rows, NT)
    plain = plain[:WIDTH] + plain[WIDTH:]
    plain = plain[:, :LANES] + plain[:, LANES:]
    cross = cross[:, :LANES] + cross[:, LANES:]
    first = cross[:WIDTH] + cross[WIDTH : 2 * WIDTH]
    second = cross[2 * WIDTH : 3 * WIDTH] + cross[3 * WIDTH :]
    cross = first[:, :WIDTH] + second[:, WIDTH:]
    gram = gram[:WIDTH] + (gram[WIDTH : 2 * WIDTH] + gram[2 * WIDTH :])
    gram = gram[:, :WIDTH] + (gram[:, WIDTH : 2 * WIDTH] + gram[:, 2 * WIDTH :])
    joined = jnp.concatenate([plain, cross, gram], axis=1)
    for y in range(4):
        out_ref[y] = joined


def left_parts(joined, matrix):
    return pl.pallas_call(
        terms_kernel,
        in_specs=in_vmem(2),
        out_specs=in_vmem(1)[0],
        out_shape=pltpu.VMEM((4, WIDTH, 2 * LANES), jnp.float32),
        compiler_params=ROOM,
        name="terms",
    )(joined, matrix)


def make_factor(gram):
    size_b = gram.shape[0]
    down = lax.broadcasted_iota(jnp.int32, (size_b, size_b), 0)
    across = lax.broadcasted_iota(jnp.int32, (size_b, size_b), 1)
    identity = jnp.where(down == across, 1.0, 0.0)
    half = 0.5 * jnp.where(down == across, gram, 0.0)
    half_down = jnp.sum(half, axis=1, keepdims=True)
    half_across = jnp.sum(half, axis=0, keepdims=True)
    scaled = jnp.where(across > down, gram, 0.0) / half_down
    inverse = identity - scaled
    powered = scaled
    for level in range((size_b - 1).bit_length() - 1):
        powered = exact(powered, powered, NN)
        inverse = exact(inverse, identity + powered, NN)
    return inverse / half_across


def last_kernel(parts_ref, columns_ref, joined_ref, matrix_ref, out_ref, done_ref, sems):
    total = (parts_ref[0] + parts_ref[1]) + (parts_ref[2] + parts_ref[3])
    factor = make_factor(total[:, LANES + WIDTH :])
    right = exact(factor, columns_ref[...], NN)
    left = total[:, :LANES] - exact(total[:, LANES : LANES + WIDTH], right, NN)
    left = exact(factor, left, TN)
    high, low = split(jnp.concatenate([doubled(right), doubled(left)], axis=0))
    copies = []
    for unit in range(16):
        rows = [reflector_block(joined_ref, unit, half) for half in range(2)]
        rows = jnp.concatenate(rows, axis=0).T
        left = split(jnp.concatenate([value_unit(joined_ref, unit), rows], axis=1))
        change = dot(left[0], high, NN) + (dot(left[0], low, NN) + dot(left[1], high, NN))
        for half in range(2):
            start = (2 * unit + half) * LANES
            span = slice(start, start + LANES)
            done_ref[span, :] = matrix_ref[span, :] - change[:, half * LANES : (half + 1) * LANES]
        if unit % 4 == 3:
            part = pl.ds((unit - 3) * 2 * LANES, 8 * LANES)
            copy = pltpu.make_async_copy(done_ref.at[part], out_ref.at[part], sems.at[unit // 4])
            copy.start()
            copies.append(copy)
    for copy in copies:
        copy.wait()


def last_step(parts, columns, joined, matrix):
    return pl.pallas_call(
        last_kernel,
        in_specs=in_vmem(4),
        out_specs=pl.BlockSpec(memory_space=pl.ANY),
        out_shape=jax.ShapeDtypeStruct(matrix.shape, jnp.float32),
        scratch_shapes=[
            pltpu.VMEM(matrix.shape, jnp.float32),
            pltpu.SemaphoreType.DMA((4,)),
        ],
        compiler_params=ROOM,
        name="last",
    )(parts, columns, joined, matrix)


def on_device(matrix, vectors):
    width, piece = vectors.shape
    core, x = lax.axis_index("core"), lax.axis_index("x")
    masked = mask_vectors(vectors, lax.axis_index(("row", "zh", "zl")) * piece)
    half = lax.dynamic_slice_in_dim(masked, core * LANES, LANES, 1)
    columns = lax.ppermute(half, AXES, column_routes())
    lines = lax.dynamic_slice_in_dim(masked, (core * 4 + x) * 8, 8, 0)
    lines = lines.reshape(8, 2, LANES).swapaxes(0, 1).reshape(16, LANES)

    matrix, columns = local(matrix), local(columns)
    values = partial_value(columns, matrix)
    values = swapped(values.reshape(2, 16, WIDTH, LANES), "core").sum(axis=0)
    values = swapped(values, PLANE).sum(axis=0)
    far = shared(jnp.concatenate([values, lines], axis=0), "zh")
    summed = far[:, :WIDTH].sum(axis=0)
    own = jnp.concatenate([summed, far[:, WIDTH:].reshape(WIDTH, LANES)], axis=0)
    joined = shared(shared(own, PLANE), "core")
    joined = local(joined.reshape(2, 4, 4, 2 * WIDTH, LANES))

    parts = local(swapped(left_parts(joined, matrix), "row"))
    return last_step(parts, columns, joined, matrix)


def solution(mesh):
    torus = Mesh(mesh.devices.reshape(4, 4, 4, 4, 2), AXES)
    placed = (P("row", COLUMNS), P(None, ("row", "zh", "zl")))
    return jax.shard_map(
        on_device, mesh=torus, in_specs=placed, out_specs=P("row", COLUMNS), check_vma=False
    )
```

```python
import jax
import jax.numpy as jnp
from jax import lax
from jax.experimental import pallas as pl
from jax.experimental.pallas import tpu as pltpu
from jax.sharding import Mesh
from jax.sharding import PartitionSpec as P

AXES = ("row", "zh", "zl", "x", "core")
COLUMNS = ("zh", "zl", "x", "core")
PLANE = ("zl", "x")
LANES = 128
WIDTH = 64
ROOM = pltpu.CompilerParams(vmem_limit_bytes=16 * 1024 * 1024)

highest = lax.Precision.HIGHEST
NN = ((1,), (0,))
NT = ((1,), (1,))
TN = ((0,), (0,))


def exact(left, right, dims):
    return lax.dot_general(
        left, right, (dims, ((), ())), precision=highest, preferred_element_type=jnp.float32
    )


def split(array):
    high = array.astype(jnp.bfloat16)
    return high, (array - high.astype(jnp.float32)).astype(jnp.bfloat16)


def dot(left, right, dims):
    return lax.dot_general(left, right, (dims, ((), ())), preferred_element_type=jnp.float32)


def swapped(array, axes):
    return lax.all_to_all(array, axes, 0, 0, tiled=True)


def shared(array, axes):
    return swapped(jnp.broadcast_to(array, (lax.axis_size(axes), *array.shape)), axes)


def mask_vectors(values, first_row):
    panel_width, row_count = values.shape
    positions = first_row + lax.iota(jnp.int32, row_count)[None, :]
    reflector = lax.iota(jnp.int32, panel_width)[:, None]
    filler = jnp.where(positions == reflector + 1, 1.0, 0.0).astype(values.dtype)
    return jnp.where(positions > reflector + 1, values, filler)


def column_routes():
    turn = {0: 2, 1: 1, 2: 0, 3: 3}
    pairs = []
    for y in range(4):
        for z in range(16):
            for x in range(4):
                for core in range(2):
                    to_x, to_z = z % 4, y * 4 + z // 4
                    to_y = (y + turn[(x - to_x) % 4]) % 4
                    here = ((y * 16 + z) * 4 + x) * 2 + core
                    pairs.append((here, ((to_y * 16 + to_z) * 4 + to_x) * 2 + core))
    return pairs


def doubled(array):
    blank = jnp.zeros_like(array)
    return jnp.concatenate(
        [jnp.concatenate([array, blank], axis=1), jnp.concatenate([blank, array], axis=1)], axis=0
    )


def local(array):
    return pltpu.with_memory_space_constraint(array, pltpu.VMEM)


def in_vmem(count):
    return [pl.BlockSpec(memory_space=pltpu.VMEM)] * count


def staging_kernel(matrix_ref, out_ref, sem):
    copy = pltpu.make_async_copy(matrix_ref, out_ref, sem)
    copy.start()
    copy.wait()


def staged(matrix):
    return pl.pallas_call(
        staging_kernel,
        in_specs=[pl.BlockSpec(memory_space=pltpu.HBM)],
        out_specs=in_vmem(1)[0],
        out_shape=pltpu.VMEM(matrix.shape, jnp.float32),
        scratch_shapes=[pltpu.SemaphoreType.DMA],
        compiler_params=ROOM,
        name="staging",
    )(pltpu.with_memory_space_constraint(matrix, pltpu.HBM))


def pair_kernel(pair_ref, out_ref):
    out_ref[...] = pair_ref[0] + pair_ref[1]


def pair_summed(pair):
    return pl.pallas_call(
        pair_kernel,
        in_specs=in_vmem(1),
        out_specs=in_vmem(1)[0],
        out_shape=pltpu.VMEM(pair.shape[1:], jnp.float32),
        compiler_params=ROOM,
        name="pair",
    )(local(pair))


def value_kernel(columns_ref, matrix_ref, out_ref):
    high, low = split(doubled(columns_ref[...].T))
    right = jnp.concatenate([high, low], axis=1)
    for unit in range(16):
        first = matrix_ref[2 * unit * LANES : (2 * unit + 1) * LANES, :]
        second = matrix_ref[(2 * unit + 1) * LANES : (2 * unit + 2) * LANES, :]
        high, low = split(jnp.concatenate([first, second], axis=1))
        both = dot(high, right, NN) + dot(low, right, NN)
        total = both[:, :LANES] + both[:, LANES:]
        out_ref[2 * unit : 2 * unit + 2] = total.reshape(2, WIDTH, LANES)


def partial_value(columns, matrix):
    return pl.pallas_call(
        value_kernel,
        in_specs=in_vmem(2),
        out_specs=in_vmem(1)[0],
        out_shape=pltpu.VMEM((32, WIDTH, LANES), jnp.float32),
        compiler_params=ROOM,
        name="value",
    )(columns, matrix)


def reflector_block(joined_ref, unit, half):
    zh, zl = divmod(unit, 4)
    start = WIDTH + zh * 16 + half * 8
    return joined_ref[:, zl, :, start : start + 8, :].reshape(WIDTH, LANES)


def value_unit(joined_ref, unit):
    piece = 2 * unit
    core, zl, x = piece // 16, piece // 4 % 4, piece % 4
    return joined_ref[core, zl, x : x + 2, :WIDTH, :].reshape(2 * WIDTH, LANES)


def in_three(array):
    high, low = split(array)
    rest = array - high.astype(jnp.float32) - low.astype(jnp.float32)
    return jnp.concatenate([high, low, rest.astype(jnp.bfloat16)], axis=0)


def terms_kernel(joined_ref, matrix_ref, out_ref):
    plain = jnp.zeros((2 * WIDTH, 2 * LANES), jnp.float32)
    cross = jnp.zeros((4 * WIDTH, 2 * LANES), jnp.float32)
    gram = jnp.zeros((3 * WIDTH, 3 * WIDTH), jnp.float32)
    for unit in range(16):
        rows = [reflector_block(joined_ref, unit, half) for half in range(2)]
        rows = in_three(jnp.concatenate(rows, axis=1))
        span = slice(2 * unit * LANES, 2 * (unit + 1) * LANES)
        right = jnp.concatenate(split(matrix_ref[span, :]), axis=1)
        plain += dot(rows[: 2 * WIDTH], right, NN)
        right = jnp.concatenate(split(value_unit(joined_ref, unit)), axis=1)
        both = [rows[: 2 * WIDTH, :LANES], rows[: 2 * WIDTH, LANES:]]
        cross += dot(jnp.concatenate(both, axis=0), right, NN)
        gram += dot(rows, rows, NT)
    plain = plain[:WIDTH] + plain[WIDTH:]
    plain = plain[:, :LANES] + plain[:, LANES:]
    cross = cross[:, :LANES] + cross[:, LANES:]
    first = cross[:WIDTH] + cross[WIDTH : 2 * WIDTH]
    second = cross[2 * WIDTH : 3 * WIDTH] + cross[3 * WIDTH :]
    cross = first[:, :WIDTH] + second[:, WIDTH:]
    gram = gram[:WIDTH] + (gram[WIDTH : 2 * WIDTH] + gram[2 * WIDTH :])
    gram = gram[:, :WIDTH] + (gram[:, WIDTH : 2 * WIDTH] + gram[:, 2 * WIDTH :])
    joined = jnp.concatenate([plain, cross, gram], axis=1)
    for y in range(4):
        out_ref[y] = joined


def left_parts(joined, matrix):
    return pl.pallas_call(
        terms_kernel,
        in_specs=in_vmem(2),
        out_specs=in_vmem(1)[0],
        out_shape=pltpu.VMEM((4, WIDTH, 2 * LANES), jnp.float32),
        compiler_params=ROOM,
        name="terms",
    )(joined, matrix)


def make_factor(gram):
    size_b = gram.shape[0]
    down = lax.broadcasted_iota(jnp.int32, (size_b, size_b), 0)
    across = lax.broadcasted_iota(jnp.int32, (size_b, size_b), 1)
    identity = jnp.where(down == across, 1.0, 0.0)
    half = 0.5 * jnp.where(down == across, gram, 0.0)
    half_down = jnp.sum(half, axis=1, keepdims=True)
    half_across = jnp.sum(half, axis=0, keepdims=True)
    scaled = jnp.where(across > down, gram, 0.0) / half_down
    inverse = identity - scaled
    powered = scaled
    for level in range((size_b - 1).bit_length() - 1):
        powered = exact(powered, powered, NN)
        inverse = exact(inverse, identity + powered, NN)
    return inverse / half_across


def last_kernel(parts_ref, columns_ref, joined_ref, matrix_ref, out_ref, done_ref, sems):
    total = (parts_ref[0] + parts_ref[1]) + (parts_ref[2] + parts_ref[3])
    factor = make_factor(total[:, LANES + WIDTH :])
    right = exact(factor, columns_ref[...], NN)
    left = total[:, :LANES] - exact(total[:, LANES : LANES + WIDTH], right, NN)
    left = exact(factor, left, TN)
    high, low = split(jnp.concatenate([doubled(right), doubled(left)], axis=0))
    copies = []
    for unit in range(16):
        rows = [reflector_block(joined_ref, unit, half) for half in range(2)]
        rows = jnp.concatenate(rows, axis=0).T
        left = split(jnp.concatenate([value_unit(joined_ref, unit), rows], axis=1))
        change = dot(left[0], high, NN) + (dot(left[0], low, NN) + dot(left[1], high, NN))
        for half in range(2):
            start = (2 * unit + half) * LANES
            span = slice(start, start + LANES)
            done_ref[span, :] = matrix_ref[span, :] - change[:, half * LANES : (half + 1) * LANES]
        if unit % 4 == 3:
            part = pl.ds((unit - 3) * 2 * LANES, 8 * LANES)
            copy = pltpu.make_async_copy(done_ref.at[part], out_ref.at[part], sems.at[unit // 4])
            copy.start()
            copies.append(copy)
    for copy in copies:
        copy.wait()


def last_step(parts, columns, joined, matrix):
    return pl.pallas_call(
        last_kernel,
        in_specs=in_vmem(4),
        out_specs=pl.BlockSpec(memory_space=pl.ANY),
        out_shape=jax.ShapeDtypeStruct(matrix.shape, jnp.float32),
        scratch_shapes=[
            pltpu.VMEM(matrix.shape, jnp.float32),
            pltpu.SemaphoreType.DMA((4,)),
        ],
        compiler_params=ROOM,
        name="last",
    )(parts, columns, joined, matrix)


def on_device(matrix, vectors):
    width, piece = vectors.shape
    core, x = lax.axis_index("core"), lax.axis_index("x")
    masked = mask_vectors(vectors, lax.axis_index(("row", "zh", "zl")) * piece)
    half = lax.dynamic_slice_in_dim(masked, core * LANES, LANES, 1)
    columns = lax.ppermute(half, AXES, column_routes())
    lines = lax.dynamic_slice_in_dim(masked, (core * 4 + x) * 8, 8, 0)
    lines = lines.reshape(8, 2, LANES).swapaxes(0, 1).reshape(16, LANES)

    matrix, columns = staged(matrix), local(columns)
    values = partial_value(columns, matrix)
    values = pair_summed(swapped(values.reshape(2, 16, WIDTH, LANES), "core"))
    values, lines = lax.optimization_barrier((values, lines))
    values = swapped(values, PLANE).sum(axis=0)
    far = shared(jnp.concatenate([values, lines], axis=0), "zh")
    summed = far[:, :WIDTH].sum(axis=0)
    own = jnp.concatenate([summed, far[:, WIDTH:].reshape(WIDTH, LANES)], axis=0)
    joined = shared(shared(own, PLANE), "core")
    joined = local(joined.reshape(2, 4, 4, 2 * WIDTH, LANES))

    parts = local(swapped(left_parts(joined, matrix), "row"))
    return last_step(parts, columns, joined, matrix)


def solution(mesh):
    torus = Mesh(mesh.devices.reshape(4, 4, 4, 4, 2), AXES)
    placed = (P("row", COLUMNS), P(None, ("row", "zh", "zl")))
    return jax.shard_map(
        on_device, mesh=torus, in_specs=placed, out_specs=P("row", COLUMNS), check_vma=False
    )
```

```python
import jax
import jax.numpy as jnp
from jax import lax
from jax.experimental import pallas as pl
from jax.experimental.pallas import tpu as pltpu
from jax.sharding import Mesh
from jax.sharding import PartitionSpec as P

AXES = ("row", "zh", "zl", "x", "core")
COLUMNS = ("zh", "zl", "x", "core")
PLANE = ("zl", "x")
LANES = 128
WIDTH = 64
ROOM = pltpu.CompilerParams(vmem_limit_bytes=16 * 1024 * 1024)

highest = lax.Precision.HIGHEST
NN = ((1,), (0,))
NT = ((1,), (1,))
TN = ((0,), (0,))


def exact(left, right, dims):
    return lax.dot_general(
        left, right, (dims, ((), ())), precision=highest, preferred_element_type=jnp.float32
    )


def split(array):
    high = array.astype(jnp.bfloat16)
    return high, (array - high.astype(jnp.float32)).astype(jnp.bfloat16)


def dot(left, right, dims):
    return lax.dot_general(left, right, (dims, ((), ())), preferred_element_type=jnp.float32)


def swapped(array, axes):
    return lax.all_to_all(array, axes, 0, 0, tiled=True)


def shared(array, axes):
    return swapped(jnp.broadcast_to(array, (lax.axis_size(axes), *array.shape)), axes)


def mask_vectors(values, first_row):
    panel_width, row_count = values.shape
    positions = first_row + lax.iota(jnp.int32, row_count)[None, :]
    reflector = lax.iota(jnp.int32, panel_width)[:, None]
    filler = jnp.where(positions == reflector + 1, 1.0, 0.0).astype(values.dtype)
    return jnp.where(positions > reflector + 1, values, filler)


def column_routes():
    turn = {0: 2, 1: 1, 2: 0, 3: 3}
    pairs = []
    for y in range(4):
        for z in range(16):
            for x in range(4):
                for core in range(2):
                    to_x, to_z = z % 4, y * 4 + z // 4
                    to_y = (y + turn[(x - to_x) % 4]) % 4
                    here = ((y * 16 + z) * 4 + x) * 2 + core
                    pairs.append((here, ((to_y * 16 + to_z) * 4 + to_x) * 2 + core))
    return pairs


def doubled(array):
    blank = jnp.zeros_like(array)
    return jnp.concatenate(
        [jnp.concatenate([array, blank], axis=1), jnp.concatenate([blank, array], axis=1)], axis=0
    )


def local(array):
    return pltpu.with_memory_space_constraint(array, pltpu.VMEM)


def in_vmem(count):
    return [pl.BlockSpec(memory_space=pltpu.VMEM)] * count


def staging_kernel(matrix_ref, out_ref, sem):
    copy = pltpu.make_async_copy(matrix_ref, out_ref, sem)
    copy.start()
    copy.wait()


def staged(matrix):
    return pl.pallas_call(
        staging_kernel,
        in_specs=[pl.BlockSpec(memory_space=pltpu.HBM)],
        out_specs=in_vmem(1)[0],
        out_shape=pltpu.VMEM(matrix.shape, jnp.float32),
        scratch_shapes=[pltpu.SemaphoreType.DMA],
        compiler_params=ROOM,
        name="staging",
    )(pltpu.with_memory_space_constraint(matrix, pltpu.HBM))


def pair_kernel(pair_ref, out_ref):
    out_ref[...] = pair_ref[0] + pair_ref[1]


def pair_summed(pair):
    return pl.pallas_call(
        pair_kernel,
        in_specs=in_vmem(1),
        out_specs=in_vmem(1)[0],
        out_shape=pltpu.VMEM(pair.shape[1:], jnp.float32),
        compiler_params=ROOM,
        name="pair",
    )(local(pair))


def value_kernel(columns_ref, matrix_ref, out_ref):
    high, low = split(doubled(columns_ref[...].T))
    right = jnp.concatenate([high, low], axis=1)
    for unit in range(16):
        first = matrix_ref[2 * unit * LANES : (2 * unit + 1) * LANES, :]
        second = matrix_ref[(2 * unit + 1) * LANES : (2 * unit + 2) * LANES, :]
        high, low = split(jnp.concatenate([first, second], axis=1))
        both = dot(high, right, NN) + dot(low, right, NN)
        total = both[:, :LANES] + both[:, LANES:]
        out_ref[2 * unit : 2 * unit + 2] = total.reshape(2, WIDTH, LANES)


def partial_value(columns, matrix):
    return pl.pallas_call(
        value_kernel,
        in_specs=in_vmem(2),
        out_specs=in_vmem(1)[0],
        out_shape=pltpu.VMEM((32, WIDTH, LANES), jnp.float32),
        compiler_params=ROOM,
        name="value",
    )(columns, matrix)


def reflector_block(joined_ref, unit, half):
    zh, zl = divmod(unit, 4)
    start = WIDTH + zh * 16 + half * 8
    return joined_ref[:, :, zl, start : start + 8, :].reshape(WIDTH, LANES)


def value_unit(joined_ref, unit):
    piece = 2 * unit
    core, zl, x = piece // 16, piece // 4 % 4, piece % 4
    return joined_ref[core, x : x + 2, zl, :WIDTH, :].reshape(2 * WIDTH, LANES)


def in_three(array):
    high, low = split(array)
    rest = array - high.astype(jnp.float32) - low.astype(jnp.float32)
    return jnp.concatenate([high, low, rest.astype(jnp.bfloat16)], axis=0)


def terms_kernel(joined_ref, matrix_ref, out_ref):
    plain = jnp.zeros((2 * WIDTH, 2 * LANES), jnp.float32)
    cross = jnp.zeros((4 * WIDTH, 2 * LANES), jnp.float32)
    gram = jnp.zeros((3 * WIDTH, 3 * WIDTH), jnp.float32)
    for unit in range(16):
        rows = [reflector_block(joined_ref, unit, half) for half in range(2)]
        rows = in_three(jnp.concatenate(rows, axis=1))
        span = slice(2 * unit * LANES, 2 * (unit + 1) * LANES)
        right = jnp.concatenate(split(matrix_ref[span, :]), axis=1)
        plain += dot(rows[: 2 * WIDTH], right, NN)
        right = jnp.concatenate(split(value_unit(joined_ref, unit)), axis=1)
        both = [rows[: 2 * WIDTH, :LANES], rows[: 2 * WIDTH, LANES:]]
        cross += dot(jnp.concatenate(both, axis=0), right, NN)
        gram += dot(rows, rows, NT)
    plain = plain[:WIDTH] + plain[WIDTH:]
    plain = plain[:, :LANES] + plain[:, LANES:]
    cross = cross[:, :LANES] + cross[:, LANES:]
    first = cross[:WIDTH] + cross[WIDTH : 2 * WIDTH]
    second = cross[2 * WIDTH : 3 * WIDTH] + cross[3 * WIDTH :]
    cross = first[:, :WIDTH] + second[:, WIDTH:]
    gram = gram[:WIDTH] + (gram[WIDTH : 2 * WIDTH] + gram[2 * WIDTH :])
    gram = gram[:, :WIDTH] + (gram[:, WIDTH : 2 * WIDTH] + gram[:, 2 * WIDTH :])
    joined = jnp.concatenate([plain, cross, gram], axis=1)
    for y in range(4):
        out_ref[y] = joined


def left_parts(joined, matrix):
    return pl.pallas_call(
        terms_kernel,
        in_specs=in_vmem(2),
        out_specs=in_vmem(1)[0],
        out_shape=pltpu.VMEM((4, WIDTH, 2 * LANES), jnp.float32),
        compiler_params=ROOM,
        name="terms",
    )(joined, matrix)


def make_factor(gram):
    size_b = gram.shape[0]
    down = lax.broadcasted_iota(jnp.int32, (size_b, size_b), 0)
    across = lax.broadcasted_iota(jnp.int32, (size_b, size_b), 1)
    identity = jnp.where(down == across, 1.0, 0.0)
    half = 0.5 * jnp.where(down == across, gram, 0.0)
    half_down = jnp.sum(half, axis=1, keepdims=True)
    half_across = jnp.sum(half, axis=0, keepdims=True)
    scaled = jnp.where(across > down, gram, 0.0) / half_down
    inverse = identity - scaled
    powered = scaled
    for level in range((size_b - 1).bit_length() - 1):
        powered = exact(powered, powered, NN)
        inverse = exact(inverse, identity + powered, NN)
    return inverse / half_across


def last_kernel(parts_ref, columns_ref, joined_ref, matrix_ref, out_ref, done_ref, sems):
    total = (parts_ref[0] + parts_ref[1]) + (parts_ref[2] + parts_ref[3])
    factor = make_factor(total[:, LANES + WIDTH :])
    right = exact(factor, columns_ref[...], NN)
    left = total[:, :LANES] - exact(total[:, LANES : LANES + WIDTH], right, NN)
    left = exact(factor, left, TN)
    high, low = split(jnp.concatenate([doubled(right), doubled(left)], axis=0))
    copies = []
    for unit in range(16):
        rows = [reflector_block(joined_ref, unit, half) for half in range(2)]
        rows = jnp.concatenate(rows, axis=0).T
        left = split(jnp.concatenate([value_unit(joined_ref, unit), rows], axis=1))
        change = dot(left[0], high, NN) + (dot(left[0], low, NN) + dot(left[1], high, NN))
        for half in range(2):
            start = (2 * unit + half) * LANES
            span = slice(start, start + LANES)
            done_ref[span, :] = matrix_ref[span, :] - change[:, half * LANES : (half + 1) * LANES]
        if unit % 4 == 3:
            part = pl.ds((unit - 3) * 2 * LANES, 8 * LANES)
            copy = pltpu.make_async_copy(done_ref.at[part], out_ref.at[part], sems.at[unit // 4])
            copy.start()
            copies.append(copy)
    for copy in copies:
        copy.wait()


def last_step(parts, columns, joined, matrix):
    return pl.pallas_call(
        last_kernel,
        in_specs=in_vmem(4),
        out_specs=pl.BlockSpec(memory_space=pl.ANY),
        out_shape=jax.ShapeDtypeStruct(matrix.shape, jnp.float32),
        scratch_shapes=[
            pltpu.VMEM(matrix.shape, jnp.float32),
            pltpu.SemaphoreType.DMA((4,)),
        ],
        compiler_params=ROOM,
        name="last",
    )(parts, columns, joined, matrix)


def on_device(matrix, vectors):
    width, piece = vectors.shape
    core, x = lax.axis_index("core"), lax.axis_index("x")
    masked = mask_vectors(vectors, lax.axis_index(("row", "zh", "zl")) * piece)
    half = lax.dynamic_slice_in_dim(masked, core * LANES, LANES, 1)
    columns = lax.ppermute(half, AXES, column_routes())
    lines = lax.dynamic_slice_in_dim(masked, (core * 4 + x) * 8, 8, 0)
    lines = lines.reshape(8, 2, LANES).swapaxes(0, 1).reshape(16, LANES)

    matrix, columns = staged(matrix), local(columns)
    values = partial_value(columns, matrix)
    values = pair_summed(swapped(values.reshape(2, 16, WIDTH, LANES), "core"))
    values, lines = lax.optimization_barrier((values, lines))
    values = swapped(values, PLANE).sum(axis=0)
    far = shared(jnp.concatenate([values, lines], axis=0), "zh")
    summed = far[:, :WIDTH].sum(axis=0)
    own = jnp.concatenate([summed, far[:, WIDTH:].reshape(WIDTH, LANES)], axis=0)
    joined = local(shared(shared(shared(own, "zl"), "x"), "core"))

    parts = local(swapped(left_parts(joined, matrix), "row"))
    return last_step(parts, columns, joined, matrix)


def solution(mesh):
    torus = Mesh(mesh.devices.reshape(4, 4, 4, 4, 2), AXES)
    placed = (P("row", COLUMNS), P(None, ("row", "zh", "zl")))
    return jax.shard_map(
        on_device, mesh=torus, in_specs=placed, out_specs=P("row", COLUMNS), check_vma=False
    )
```

```python
import jax
import jax.numpy as jnp
from jax import lax
from jax.experimental import pallas as pl
from jax.experimental.pallas import tpu as pltpu
from jax.sharding import Mesh
from jax.sharding import PartitionSpec as P

AXES = ("row", "zh", "zl", "x", "core")
COLUMNS = ("zh", "zl", "x", "core")
PLANE = ("zl", "x")
LANES = 128
WIDTH = 64
ROOM = pltpu.CompilerParams(vmem_limit_bytes=16 * 1024 * 1024)

highest = lax.Precision.HIGHEST
NN = ((1,), (0,))
NT = ((1,), (1,))
TN = ((0,), (0,))


def exact(left, right, dims):
    return lax.dot_general(
        left, right, (dims, ((), ())), precision=highest, preferred_element_type=jnp.float32
    )


def split(array):
    high = array.astype(jnp.bfloat16)
    return high, (array - high.astype(jnp.float32)).astype(jnp.bfloat16)


def dot(left, right, dims):
    return lax.dot_general(left, right, (dims, ((), ())), preferred_element_type=jnp.float32)


def swapped(array, axes):
    return lax.all_to_all(array, axes, 0, 0, tiled=True)


def shared(array, axes):
    return swapped(jnp.broadcast_to(array, (lax.axis_size(axes), *array.shape)), axes)


def mask_vectors(values, first_row):
    panel_width, row_count = values.shape
    positions = first_row + lax.iota(jnp.int32, row_count)[None, :]
    reflector = lax.iota(jnp.int32, panel_width)[:, None]
    filler = jnp.where(positions == reflector + 1, 1.0, 0.0).astype(values.dtype)
    return jnp.where(positions > reflector + 1, values, filler)


def column_routes():
    turn = {0: 2, 1: 1, 2: 0, 3: 3}
    pairs = []
    for y in range(4):
        for z in range(16):
            for x in range(4):
                for core in range(2):
                    to_x, to_z = z % 4, y * 4 + z // 4
                    to_y = (y + turn[(x - to_x) % 4]) % 4
                    here = ((y * 16 + z) * 4 + x) * 2 + core
                    pairs.append((here, ((to_y * 16 + to_z) * 4 + to_x) * 2 + core))
    return pairs


def doubled(array):
    blank = jnp.zeros_like(array)
    return jnp.concatenate(
        [jnp.concatenate([array, blank], axis=1), jnp.concatenate([blank, array], axis=1)], axis=0
    )


def local(array):
    return pltpu.with_memory_space_constraint(array, pltpu.VMEM)


def in_vmem(count):
    return [pl.BlockSpec(memory_space=pltpu.VMEM)] * count


def value_kernel(piece_ref, halves_ref, out_ref):
    right = []
    for half in range(2):
        columns = piece_ref[:, half * LANES : (half + 1) * LANES].T
        right.append(jnp.concatenate(split(doubled(columns)), axis=1))
    for unit in range(8):
        both = jnp.zeros((LANES, 2 * LANES), jnp.float32)
        for half in range(2):
            first = halves_ref[half, 2 * unit * LANES : (2 * unit + 1) * LANES, :]
            second = halves_ref[half, (2 * unit + 1) * LANES : (2 * unit + 2) * LANES, :]
            high, low = split(jnp.concatenate([first, second], axis=1))
            both += dot(high, right[half], NN) + dot(low, right[half], NN)
        total = both[:, :LANES] + both[:, LANES:]
        out_ref[2 * unit : 2 * unit + 2] = total.reshape(2, WIDTH, LANES)


def half_value(piece, halves):
    return pl.pallas_call(
        value_kernel,
        in_specs=in_vmem(2),
        out_specs=in_vmem(1)[0],
        out_shape=pltpu.VMEM((16, WIDTH, LANES), jnp.float32),
        compiler_params=ROOM,
        name="value",
    )(local(piece), local(halves))


def reflector_block(joined_ref, unit, half):
    zh, zl = divmod(unit, 4)
    start = WIDTH + zh * 16 + half * 8
    return joined_ref[:, :, zl, start : start + 8, :].reshape(WIDTH, LANES)


def value_unit(joined_ref, unit):
    piece = 2 * unit
    core, zl, x = piece // 16, piece // 4 % 4, piece % 4
    return joined_ref[core, x : x + 2, zl, :WIDTH, :].reshape(2 * WIDTH, LANES)


def in_three(array):
    high, low = split(array)
    rest = array - high.astype(jnp.float32) - low.astype(jnp.float32)
    return jnp.concatenate([high, low, rest.astype(jnp.bfloat16)], axis=0)


def terms_kernel(joined_ref, matrix_ref, out_ref):
    plain = jnp.zeros((2 * WIDTH, 2 * LANES), jnp.float32)
    cross = jnp.zeros((4 * WIDTH, 2 * LANES), jnp.float32)
    gram = jnp.zeros((3 * WIDTH, 3 * WIDTH), jnp.float32)
    for unit in range(16):
        rows = [reflector_block(joined_ref, unit, half) for half in range(2)]
        rows = in_three(jnp.concatenate(rows, axis=1))
        span = slice(2 * unit * LANES, 2 * (unit + 1) * LANES)
        right = jnp.concatenate(split(matrix_ref[span, :]), axis=1)
        plain += dot(rows[: 2 * WIDTH], right, NN)
        right = jnp.concatenate(split(value_unit(joined_ref, unit)), axis=1)
        both = [rows[: 2 * WIDTH, :LANES], rows[: 2 * WIDTH, LANES:]]
        cross += dot(jnp.concatenate(both, axis=0), right, NN)
        gram += dot(rows, rows, NT)
    plain = plain[:WIDTH] + plain[WIDTH:]
    plain = plain[:, :LANES] + plain[:, LANES:]
    cross = cross[:, :LANES] + cross[:, LANES:]
    first = cross[:WIDTH] + cross[WIDTH : 2 * WIDTH]
    second = cross[2 * WIDTH : 3 * WIDTH] + cross[3 * WIDTH :]
    cross = first[:, :WIDTH] + second[:, WIDTH:]
    gram = gram[:WIDTH] + (gram[WIDTH : 2 * WIDTH] + gram[2 * WIDTH :])
    gram = gram[:, :WIDTH] + (gram[:, WIDTH : 2 * WIDTH] + gram[:, 2 * WIDTH :])
    joined = jnp.concatenate([plain, cross, gram], axis=1)
    for y in range(4):
        out_ref[y] = joined


def left_parts(joined, matrix):
    return pl.pallas_call(
        terms_kernel,
        in_specs=in_vmem(2),
        out_specs=in_vmem(1)[0],
        out_shape=pltpu.VMEM((4, WIDTH, 2 * LANES), jnp.float32),
        compiler_params=ROOM,
        name="terms",
    )(joined, matrix)


def make_factor(gram):
    size_b = gram.shape[0]
    down = lax.broadcasted_iota(jnp.int32, (size_b, size_b), 0)
    across = lax.broadcasted_iota(jnp.int32, (size_b, size_b), 1)
    identity = jnp.where(down == across, 1.0, 0.0)
    half = 0.5 * jnp.where(down == across, gram, 0.0)
    half_down = jnp.sum(half, axis=1, keepdims=True)
    half_across = jnp.sum(half, axis=0, keepdims=True)
    scaled = jnp.where(across > down, gram, 0.0) / half_down
    inverse = identity - scaled
    powered = scaled
    for level in range((size_b - 1).bit_length() - 1):
        powered = exact(powered, powered, NN)
        inverse = exact(inverse, identity + powered, NN)
    return inverse / half_across


def last_kernel(parts_ref, columns_ref, joined_ref, matrix_ref, out_ref, done_ref, sems):
    total = (parts_ref[0] + parts_ref[1]) + (parts_ref[2] + parts_ref[3])
    factor = make_factor(total[:, LANES + WIDTH :])
    right = exact(factor, columns_ref[...], NN)
    left = total[:, :LANES] - exact(total[:, LANES : LANES + WIDTH], right, NN)
    left = exact(factor, left, TN)
    high, low = split(jnp.concatenate([doubled(right), doubled(left)], axis=0))
    copies = []
    for unit in range(16):
        rows = [reflector_block(joined_ref, unit, half) for half in range(2)]
        rows = jnp.concatenate(rows, axis=0).T
        left = split(jnp.concatenate([value_unit(joined_ref, unit), rows], axis=1))
        change = dot(left[0], high, NN) + (dot(left[0], low, NN) + dot(left[1], high, NN))
        for half in range(2):
            start = (2 * unit + half) * LANES
            span = slice(start, start + LANES)
            done_ref[span, :] = matrix_ref[span, :] - change[:, half * LANES : (half + 1) * LANES]
        if unit % 4 == 3:
            part = pl.ds((unit - 3) * 2 * LANES, 8 * LANES)
            copy = pltpu.make_async_copy(done_ref.at[part], out_ref.at[part], sems.at[unit // 4])
            copy.start()
            copies.append(copy)
    for copy in copies:
        copy.wait()


def last_step(parts, columns, joined, matrix):
    return pl.pallas_call(
        last_kernel,
        in_specs=in_vmem(4),
        out_specs=pl.BlockSpec(memory_space=pl.ANY),
        out_shape=jax.ShapeDtypeStruct(matrix.shape, jnp.float32),
        scratch_shapes=[
            pltpu.VMEM(matrix.shape, jnp.float32),
            pltpu.SemaphoreType.DMA((4,)),
        ],
        compiler_params=ROOM,
        name="last",
    )(parts, columns, joined, matrix)


def on_device(matrix, vectors):
    width, span = vectors.shape
    core, x = lax.axis_index("core"), lax.axis_index("x")
    halves = swapped(matrix.reshape(2, -1, LANES), "core")
    piece = lax.ppermute(vectors, AXES, column_routes())
    matrix = local(matrix)
    masked = mask_vectors(vectors, lax.axis_index(("row", "zh", "zl")) * span)
    lines = lax.dynamic_slice_in_dim(masked, (core * 4 + x) * 8, 8, 0)
    lines = lines.reshape(8, 2, LANES).swapaxes(0, 1).reshape(16, LANES)

    piece = mask_vectors(piece, lax.axis_index(("zh", "zl", "x")) * span)
    columns = local(lax.dynamic_slice_in_dim(piece, core * LANES, LANES, 1))
    values = half_value(piece, halves)
    values, lines, columns = lax.optimization_barrier((values, lines, columns))
    values = swapped(values, PLANE).sum(axis=0)
    far = shared(jnp.concatenate([values, lines], axis=0), "zh")
    summed = far[:, :WIDTH].sum(axis=0)
    own = jnp.concatenate([summed, far[:, WIDTH:].reshape(WIDTH, LANES)], axis=0)
    joined = local(shared(shared(shared(own, "zl"), "x"), "core"))

    parts = local(swapped(left_parts(joined, matrix), "row"))
    return last_step(parts, columns, joined, matrix)


def solution(mesh):
    torus = Mesh(mesh.devices.reshape(4, 4, 4, 4, 2), AXES)
    placed = (P("row", COLUMNS), P(None, ("row", "zh", "zl")))
    return jax.shard_map(
        on_device, mesh=torus, in_specs=placed, out_specs=P("row", COLUMNS), check_vma=False
    )
```

```python
import jax
import jax.numpy as jnp
from jax import lax
from jax.experimental import pallas as pl
from jax.experimental.pallas import tpu as pltpu
from jax.sharding import Mesh
from jax.sharding import PartitionSpec as P

AXES = ("row", "zh", "zl", "x", "core")
COLUMNS = ("zh", "zl", "x", "core")
LANES = 128
WIDTH = 64
ROOM = pltpu.CompilerParams(vmem_limit_bytes=16 * 1024 * 1024)

highest = lax.Precision.HIGHEST
NN = ((1,), (0,))
NT = ((1,), (1,))
TN = ((0,), (0,))


def exact(left, right, dims):
    return lax.dot_general(
        left, right, (dims, ((), ())), precision=highest, preferred_element_type=jnp.float32
    )


def split(array):
    high = array.astype(jnp.bfloat16)
    return high, (array - high.astype(jnp.float32)).astype(jnp.bfloat16)


def dot(left, right, dims):
    return lax.dot_general(left, right, (dims, ((), ())), preferred_element_type=jnp.float32)


def swapped(array, axes):
    return lax.all_to_all(array, axes, 0, 0, tiled=True)


def shared(array, axes):
    return swapped(jnp.broadcast_to(array, (lax.axis_size(axes), *array.shape)), axes)


def mask_vectors(values, first_row):
    panel_width, row_count = values.shape
    positions = first_row + lax.iota(jnp.int32, row_count)[None, :]
    reflector = lax.iota(jnp.int32, panel_width)[:, None]
    filler = jnp.where(positions == reflector + 1, 1.0, 0.0).astype(values.dtype)
    return jnp.where(positions > reflector + 1, values, filler)


def column_routes():
    turn = {0: 2, 1: 1, 2: 0, 3: 3}
    pairs = []
    for y in range(4):
        for z in range(16):
            for x in range(4):
                for core in range(2):
                    to_x, to_z = z % 4, y * 4 + z // 4
                    to_y = (y + turn[(x - to_x) % 4]) % 4
                    here = ((y * 16 + z) * 4 + x) * 2 + core
                    pairs.append((here, ((to_y * 16 + to_z) * 4 + to_x) * 2 + core))
    return pairs


def doubled(array):
    blank = jnp.zeros_like(array)
    return jnp.concatenate(
        [jnp.concatenate([array, blank], axis=1), jnp.concatenate([blank, array], axis=1)], axis=0
    )


def local(array):
    return pltpu.with_memory_space_constraint(array, pltpu.VMEM)


def in_vmem(count):
    return [pl.BlockSpec(memory_space=pltpu.VMEM)] * count


def staging_kernel(matrix_ref, out_ref, sem):
    copy = pltpu.make_async_copy(matrix_ref, out_ref, sem)
    copy.start()
    copy.wait()


def staged(matrix):
    return pl.pallas_call(
        staging_kernel,
        in_specs=[pl.BlockSpec(memory_space=pltpu.HBM)],
        out_specs=in_vmem(1)[0],
        out_shape=pltpu.VMEM(matrix.shape, jnp.float32),
        scratch_shapes=[pltpu.SemaphoreType.DMA],
        compiler_params=ROOM,
        name="staging",
    )(pltpu.with_memory_space_constraint(matrix, pltpu.HBM))


def sum_kernel(parts_ref, out_ref):
    parts = [parts_ref[k] for k in range(parts_ref.shape[0])]
    while len(parts) > 1:
        parts = [parts[k] + parts[k + 1] for k in range(0, len(parts), 2)]
    out_ref[...] = parts[0]


def summed(parts):
    return pl.pallas_call(
        sum_kernel,
        in_specs=in_vmem(1),
        out_specs=in_vmem(1)[0],
        out_shape=pltpu.VMEM(parts.shape[1:], jnp.float32),
        compiler_params=ROOM,
        name="sum",
    )(local(parts))


def staging_kernel(matrix_ref, out_ref, sem):
    copy = pltpu.make_async_copy(matrix_ref, out_ref, sem)
    copy.start()
    copy.wait()


def staged(matrix):
    return pl.pallas_call(
        staging_kernel,
        in_specs=[pl.BlockSpec(memory_space=pltpu.HBM)],
        out_specs=in_vmem(1)[0],
        out_shape=pltpu.VMEM(matrix.shape, jnp.float32),
        scratch_shapes=[pltpu.SemaphoreType.DMA],
        compiler_params=ROOM,
        name="staging",
    )(pltpu.with_memory_space_constraint(matrix, pltpu.HBM))


def pair_kernel(pair_ref, out_ref):
    out_ref[...] = pair_ref[0] + pair_ref[1]


def pair_summed(pair):
    return pl.pallas_call(
        pair_kernel,
        in_specs=in_vmem(1),
        out_specs=in_vmem(1)[0],
        out_shape=pltpu.VMEM(pair.shape[1:], jnp.float32),
        compiler_params=ROOM,
        name="pair",
    )(local(pair))


def value_kernel(columns_ref, matrix_ref, out_ref):
    high, low = split(doubled(columns_ref[...].T))
    right = jnp.concatenate([high, low], axis=1)
    for unit in range(16):
        first = matrix_ref[2 * unit * LANES : (2 * unit + 1) * LANES, :]
        second = matrix_ref[(2 * unit + 1) * LANES : (2 * unit + 2) * LANES, :]
        high, low = split(jnp.concatenate([first, second], axis=1))
        both = dot(high, right, NN) + dot(low, right, NN)
        total = both[:, :LANES] + both[:, LANES:]
        for half in range(2):
            core, zl, x = (2 * unit + half) // 16, unit // 2 % 4, (2 * unit + half) % 4
            out_ref[core, x, zl] = total[half * WIDTH : (half + 1) * WIDTH]


def partial_value(columns, matrix):
    return pl.pallas_call(
        value_kernel,
        in_specs=in_vmem(2),
        out_specs=in_vmem(1)[0],
        out_shape=pltpu.VMEM((2, 4, 4, WIDTH, LANES), jnp.float32),
        compiler_params=ROOM,
        name="value",
    )(columns, matrix)


def reflector_block(joined_ref, unit, half):
    zh, zl = divmod(unit, 4)
    start = WIDTH + zh * 16 + half * 8
    return joined_ref[:, :, zl, start : start + 8, :].reshape(WIDTH, LANES)


def value_unit(joined_ref, unit):
    piece = 2 * unit
    core, zl, x = piece // 16, piece // 4 % 4, piece % 4
    return joined_ref[core, x : x + 2, zl, :WIDTH, :].reshape(2 * WIDTH, LANES)


def in_three(array):
    high, low = split(array)
    rest = array - high.astype(jnp.float32) - low.astype(jnp.float32)
    return jnp.concatenate([high, low, rest.astype(jnp.bfloat16)], axis=0)


def terms_kernel(joined_ref, matrix_ref, out_ref):
    plain = jnp.zeros((2 * WIDTH, 2 * LANES), jnp.float32)
    cross = jnp.zeros((4 * WIDTH, 2 * LANES), jnp.float32)
    gram = jnp.zeros((3 * WIDTH, 3 * WIDTH), jnp.float32)
    for unit in range(16):
        rows = [reflector_block(joined_ref, unit, half) for half in range(2)]
        rows = in_three(jnp.concatenate(rows, axis=1))
        span = slice(2 * unit * LANES, 2 * (unit + 1) * LANES)
        right = jnp.concatenate(split(matrix_ref[span, :]), axis=1)
        plain += dot(rows[: 2 * WIDTH], right, NN)
        right = jnp.concatenate(split(value_unit(joined_ref, unit)), axis=1)
        both = [rows[: 2 * WIDTH, :LANES], rows[: 2 * WIDTH, LANES:]]
        cross += dot(jnp.concatenate(both, axis=0), right, NN)
        gram += dot(rows, rows, NT)
    plain = plain[:WIDTH] + plain[WIDTH:]
    plain = plain[:, :LANES] + plain[:, LANES:]
    cross = cross[:, :LANES] + cross[:, LANES:]
    first = cross[:WIDTH] + cross[WIDTH : 2 * WIDTH]
    second = cross[2 * WIDTH : 3 * WIDTH] + cross[3 * WIDTH :]
    cross = first[:, :WIDTH] + second[:, WIDTH:]
    gram = gram[:WIDTH] + (gram[WIDTH : 2 * WIDTH] + gram[2 * WIDTH :])
    gram = gram[:, :WIDTH] + (gram[:, WIDTH : 2 * WIDTH] + gram[:, 2 * WIDTH :])
    joined = jnp.concatenate([plain, cross, gram], axis=1)
    for y in range(4):
        out_ref[y] = joined


def left_parts(joined, matrix):
    return pl.pallas_call(
        terms_kernel,
        in_specs=in_vmem(2),
        out_specs=in_vmem(1)[0],
        out_shape=pltpu.VMEM((4, WIDTH, 2 * LANES), jnp.float32),
        compiler_params=ROOM,
        name="terms",
    )(joined, matrix)


def make_factor(gram):
    size_b = gram.shape[0]
    down = lax.broadcasted_iota(jnp.int32, (size_b, size_b), 0)
    across = lax.broadcasted_iota(jnp.int32, (size_b, size_b), 1)
    identity = jnp.where(down == across, 1.0, 0.0)
    half = 0.5 * jnp.where(down == across, gram, 0.0)
    half_down = jnp.sum(half, axis=1, keepdims=True)
    half_across = jnp.sum(half, axis=0, keepdims=True)
    scaled = jnp.where(across > down, gram, 0.0) / half_down
    inverse = identity - scaled
    powered = scaled
    for level in range((size_b - 1).bit_length() - 1):
        powered = exact(powered, powered, NN)
        inverse = exact(inverse, identity + powered, NN)
    return inverse / half_across


def last_kernel(parts_ref, columns_ref, joined_ref, matrix_ref, out_ref, done_ref, sems):
    total = (parts_ref[0] + parts_ref[1]) + (parts_ref[2] + parts_ref[3])
    factor = make_factor(total[:, LANES + WIDTH :])
    right = exact(factor, columns_ref[...], NN)
    left = total[:, :LANES] - exact(total[:, LANES : LANES + WIDTH], right, NN)
    left = exact(factor, left, TN)
    high, low = split(jnp.concatenate([doubled(right), doubled(left)], axis=0))
    copies = []
    for unit in range(16):
        rows = [reflector_block(joined_ref, unit, half) for half in range(2)]
        rows = jnp.concatenate(rows, axis=0).T
        left = split(jnp.concatenate([value_unit(joined_ref, unit), rows], axis=1))
        change = dot(left[0], high, NN) + (dot(left[0], low, NN) + dot(left[1], high, NN))
        for half in range(2):
            start = (2 * unit + half) * LANES
            span = slice(start, start + LANES)
            done_ref[span, :] = matrix_ref[span, :] - change[:, half * LANES : (half + 1) * LANES]
        if unit % 4 == 3:
            part = pl.ds((unit - 3) * 2 * LANES, 8 * LANES)
            copy = pltpu.make_async_copy(done_ref.at[part], out_ref.at[part], sems.at[unit // 4])
            copy.start()
            copies.append(copy)
    for copy in copies:
        copy.wait()


def last_step(parts, columns, joined, matrix):
    return pl.pallas_call(
        last_kernel,
        in_specs=in_vmem(4),
        out_specs=pl.BlockSpec(memory_space=pl.ANY),
        out_shape=jax.ShapeDtypeStruct(matrix.shape, jnp.float32),
        scratch_shapes=[
            pltpu.VMEM(matrix.shape, jnp.float32),
            pltpu.SemaphoreType.DMA((4,)),
        ],
        compiler_params=ROOM,
        name="last",
    )(parts, columns, joined, matrix)


def on_device(matrix, vectors):
    width, piece = vectors.shape
    core, x = lax.axis_index("core"), lax.axis_index("x")
    masked = mask_vectors(vectors, lax.axis_index(("row", "zh", "zl")) * piece)
    half = lax.dynamic_slice_in_dim(masked, core * LANES, LANES, 1)
    columns = lax.ppermute(half, AXES, column_routes())
    lines = lax.dynamic_slice_in_dim(masked, (core * 4 + x) * 8, 8, 0)
    lines = lines.reshape(8, 2, LANES).swapaxes(0, 1).reshape(16, LANES)

    matrix, columns = staged(matrix), local(columns)
    values = partial_value(columns, matrix)
    values = summed(swapped(values, "core"))
    values, lines = lax.optimization_barrier((values, lines))
    values = summed(swapped(summed(swapped(values, "x")), "zl"))
    far = shared(jnp.concatenate([values, lines], axis=0), "zh")
    near = far[:, :WIDTH].sum(axis=0)
    own = jnp.concatenate([near, far[:, WIDTH:].reshape(WIDTH, LANES)], axis=0)
    joined = local(shared(shared(shared(own, "zl"), "x"), "core"))

    parts = local(swapped(left_parts(joined, matrix), "row"))
    return last_step(parts, columns, joined, matrix)


def solution(mesh):
    torus = Mesh(mesh.devices.reshape(4, 4, 4, 4, 2), AXES)
    placed = (P("row", COLUMNS), P(None, ("row", "zh", "zl")))
    return jax.shard_map(
        on_device, mesh=torus, in_specs=placed, out_specs=P("row", COLUMNS), check_vma=False
    )
```

```python
import jax
import jax.numpy as jnp
from jax import lax
from jax.experimental import pallas as pl
from jax.experimental.pallas import tpu as pltpu
from jax.sharding import Mesh
from jax.sharding import PartitionSpec as P

AXES = ("row", "zh", "zl", "x", "core")
COLUMNS = ("zh", "zl", "x", "core")
PLANE = ("zl", "x")
LANES = 128
WIDTH = 64
ROOM = pltpu.CompilerParams(vmem_limit_bytes=16 * 1024 * 1024)

highest = lax.Precision.HIGHEST
NN = ((1,), (0,))
NT = ((1,), (1,))
TN = ((0,), (0,))


def exact(left, right, dims):
    return lax.dot_general(
        left, right, (dims, ((), ())), precision=highest, preferred_element_type=jnp.float32
    )


def split(array):
    high = array.astype(jnp.bfloat16)
    return high, (array - high.astype(jnp.float32)).astype(jnp.bfloat16)


def dot(left, right, dims):
    return lax.dot_general(left, right, (dims, ((), ())), preferred_element_type=jnp.float32)


def swapped(array, axes):
    return lax.all_to_all(array, axes, 0, 0, tiled=True)


def shared(array, axes):
    return swapped(jnp.broadcast_to(array, (lax.axis_size(axes), *array.shape)), axes)


def mask_vectors(values, first_row):
    panel_width, row_count = values.shape
    positions = first_row + lax.iota(jnp.int32, row_count)[None, :]
    reflector = lax.iota(jnp.int32, panel_width)[:, None]
    filler = jnp.where(positions == reflector + 1, 1.0, 0.0).astype(values.dtype)
    return jnp.where(positions > reflector + 1, values, filler)


def column_routes():
    turn = {0: 2, 1: 1, 2: 0, 3: 3}
    pairs = []
    for y in range(4):
        for z in range(16):
            for x in range(4):
                for core in range(2):
                    to_x, to_z = z % 4, y * 4 + z // 4
                    to_y = (y + turn[(x - to_x) % 4]) % 4
                    here = ((y * 16 + z) * 4 + x) * 2 + core
                    pairs.append((here, ((to_y * 16 + to_z) * 4 + to_x) * 2 + core))
    return pairs


def doubled(array):
    blank = jnp.zeros_like(array)
    return jnp.concatenate(
        [jnp.concatenate([array, blank], axis=1), jnp.concatenate([blank, array], axis=1)], axis=0
    )


def local(array):
    return pltpu.with_memory_space_constraint(array, pltpu.VMEM)


def in_vmem(count):
    return [pl.BlockSpec(memory_space=pltpu.VMEM)] * count


def staging_kernel(matrix_ref, out_ref, sem):
    copy = pltpu.make_async_copy(matrix_ref, out_ref, sem)
    copy.start()
    copy.wait()


def staged(matrix):
    return pl.pallas_call(
        staging_kernel,
        in_specs=[pl.BlockSpec(memory_space=pltpu.HBM)],
        out_specs=in_vmem(1)[0],
        out_shape=pltpu.VMEM(matrix.shape, jnp.float32),
        scratch_shapes=[pltpu.SemaphoreType.DMA],
        compiler_params=ROOM,
        name="staging",
    )(pltpu.with_memory_space_constraint(matrix, pltpu.HBM))


def pair_kernel(pair_ref, out_ref):
    out_ref[...] = pair_ref[0] + pair_ref[1]


def pair_summed(pair):
    return pl.pallas_call(
        pair_kernel,
        in_specs=in_vmem(1),
        out_specs=in_vmem(1)[0],
        out_shape=pltpu.VMEM(pair.shape[1:], jnp.float32),
        compiler_params=ROOM,
        name="pair",
    )(local(pair))


def value_kernel(place_ref, piece_ref, matrix_ref, out_ref, columns_ref):
    start = pl.multiple_of(place_ref[0] * LANES, LANES)
    columns = mask_vectors(piece_ref[:, pl.ds(start, LANES)], place_ref[1])
    columns_ref[...] = columns
    high, low = split(doubled(columns.T))
    right = jnp.concatenate([high, low], axis=1)
    for unit in range(16):
        first = matrix_ref[2 * unit * LANES : (2 * unit + 1) * LANES, :]
        second = matrix_ref[(2 * unit + 1) * LANES : (2 * unit + 2) * LANES, :]
        high, low = split(jnp.concatenate([first, second], axis=1))
        both = dot(high, right, NN) + dot(low, right, NN)
        total = both[:, :LANES] + both[:, LANES:]
        out_ref[2 * unit : 2 * unit + 2] = total.reshape(2, WIDTH, LANES)


def partial_value(place, piece, matrix):
    return pl.pallas_call(
        value_kernel,
        in_specs=[pl.BlockSpec(memory_space=pltpu.SMEM), *in_vmem(2)],
        out_specs=in_vmem(2),
        out_shape=[
            pltpu.VMEM((32, WIDTH, LANES), jnp.float32),
            pltpu.VMEM((WIDTH, LANES), jnp.float32),
        ],
        compiler_params=ROOM,
        name="value",
    )(place, local(piece), matrix)


def reflector_block(core, own_ref, other_ref, unit, half):
    zh, zl = divmod(unit, 4)
    start = WIDTH + zh * 16 + half * 8
    own = own_ref[:, zl, start : start + 8, :].reshape(WIDTH // 2, LANES)
    other = other_ref[:, zl, start : start + 8, :].reshape(WIDTH // 2, LANES)
    first = jnp.where(core == 0, own, other)
    return jnp.concatenate([first, jnp.where(core == 0, other, own)], axis=0)


def value_unit(core, own_ref, other_ref, unit):
    piece = 2 * unit
    zl, x = piece // 4 % 4, piece % 4
    own, other = own_ref[x : x + 2, zl, :WIDTH, :], other_ref[x : x + 2, zl, :WIDTH, :]
    return jnp.where(core == piece // 16, own, other).reshape(2 * WIDTH, LANES)


def in_three(array):
    high, low = split(array)
    rest = array - high.astype(jnp.float32) - low.astype(jnp.float32)
    return jnp.concatenate([high, low, rest.astype(jnp.bfloat16)], axis=0)


def terms_kernel(place_ref, own_ref, other_ref, matrix_ref, out_ref):
    held = (place_ref[0], own_ref, other_ref)
    plain = jnp.zeros((2 * WIDTH, 2 * LANES), jnp.float32)
    cross = jnp.zeros((4 * WIDTH, 2 * LANES), jnp.float32)
    gram = jnp.zeros((3 * WIDTH, 3 * WIDTH), jnp.float32)
    for unit in range(16):
        rows = [reflector_block(*held, unit, half) for half in range(2)]
        rows = in_three(jnp.concatenate(rows, axis=1))
        span = slice(2 * unit * LANES, 2 * (unit + 1) * LANES)
        right = jnp.concatenate(split(matrix_ref[span, :]), axis=1)
        plain += dot(rows[: 2 * WIDTH], right, NN)
        right = jnp.concatenate(split(value_unit(*held, unit)), axis=1)
        both = [rows[: 2 * WIDTH, :LANES], rows[: 2 * WIDTH, LANES:]]
        cross += dot(jnp.concatenate(both, axis=0), right, NN)
        gram += dot(rows, rows, NT)
    plain = plain[:WIDTH] + plain[WIDTH:]
    plain = plain[:, :LANES] + plain[:, LANES:]
    cross = cross[:, :LANES] + cross[:, LANES:]
    first = cross[:WIDTH] + cross[WIDTH : 2 * WIDTH]
    second = cross[2 * WIDTH : 3 * WIDTH] + cross[3 * WIDTH :]
    cross = first[:, :WIDTH] + second[:, WIDTH:]
    gram = gram[:WIDTH] + (gram[WIDTH : 2 * WIDTH] + gram[2 * WIDTH :])
    gram = gram[:, :WIDTH] + (gram[:, WIDTH : 2 * WIDTH] + gram[:, 2 * WIDTH :])
    joined = jnp.concatenate([plain, cross, gram], axis=1)
    for y in range(4):
        out_ref[y] = joined


def left_parts(place, own, other, matrix):
    return pl.pallas_call(
        terms_kernel,
        in_specs=[pl.BlockSpec(memory_space=pltpu.SMEM), *in_vmem(3)],
        out_specs=in_vmem(1)[0],
        out_shape=pltpu.VMEM((4, WIDTH, 2 * LANES), jnp.float32),
        compiler_params=ROOM,
        name="terms",
    )(place, own, other, matrix)


def make_factor(gram):
    size_b = gram.shape[0]
    down = lax.broadcasted_iota(jnp.int32, (size_b, size_b), 0)
    across = lax.broadcasted_iota(jnp.int32, (size_b, size_b), 1)
    identity = jnp.where(down == across, 1.0, 0.0)
    half = 0.5 * jnp.where(down == across, gram, 0.0)
    half_down = jnp.sum(half, axis=1, keepdims=True)
    half_across = jnp.sum(half, axis=0, keepdims=True)
    scaled = jnp.where(across > down, gram, 0.0) / half_down
    inverse = identity - scaled
    powered = scaled
    for level in range((size_b - 1).bit_length() - 1):
        powered = exact(powered, powered, NN)
        inverse = exact(inverse, identity + powered, NN)
    return inverse / half_across


def last_kernel(
    place_ref, parts_ref, columns_ref, own_ref, other_ref, matrix_ref, out_ref, done_ref, sems
):
    held = (place_ref[0], own_ref, other_ref)
    total = (parts_ref[0] + parts_ref[1]) + (parts_ref[2] + parts_ref[3])
    factor = make_factor(total[:, LANES + WIDTH :])
    right = exact(factor, columns_ref[...], NN)
    left = total[:, :LANES] - exact(total[:, LANES : LANES + WIDTH], right, NN)
    left = exact(factor, left, TN)
    high, low = split(jnp.concatenate([doubled(right), doubled(left)], axis=0))
    copies = []
    for unit in range(16):
        rows = [reflector_block(*held, unit, half) for half in range(2)]
        rows = jnp.concatenate(rows, axis=0).T
        left = split(jnp.concatenate([value_unit(*held, unit), rows], axis=1))
        change = dot(left[0], high, NN) + (dot(left[0], low, NN) + dot(left[1], high, NN))
        for half in range(2):
            start = (2 * unit + half) * LANES
            span = slice(start, start + LANES)
            done_ref[span, :] = matrix_ref[span, :] - change[:, half * LANES : (half + 1) * LANES]
        if unit % 4 == 3:
            part = pl.ds((unit - 3) * 2 * LANES, 8 * LANES)
            copy = pltpu.make_async_copy(done_ref.at[part], out_ref.at[part], sems.at[unit // 4])
            copy.start()
            copies.append(copy)
    for copy in copies:
        copy.wait()


def last_step(place, parts, columns, own, other, matrix):
    return pl.pallas_call(
        last_kernel,
        in_specs=[pl.BlockSpec(memory_space=pltpu.SMEM), *in_vmem(5)],
        out_specs=pl.BlockSpec(memory_space=pl.ANY),
        out_shape=jax.ShapeDtypeStruct(matrix.shape, jnp.float32),
        scratch_shapes=[
            pltpu.VMEM(matrix.shape, jnp.float32),
            pltpu.SemaphoreType.DMA((4,)),
        ],
        compiler_params=ROOM,
        name="last",
    )(place, parts, columns, own, other, matrix)


def on_device(matrix, vectors):
    width, span = vectors.shape
    core, x = lax.axis_index("core"), lax.axis_index("x")
    first = lax.axis_index(("zh", "zl", "x", "core")) * LANES
    place = jnp.stack([core, first])
    piece = lax.ppermute(vectors, AXES, column_routes())
    masked = mask_vectors(vectors, lax.axis_index(("row", "zh", "zl")) * span)
    lines = lax.dynamic_slice_in_dim(masked, (core * 4 + x) * 8, 8, 0)
    lines = lines.reshape(8, 2, LANES).swapaxes(0, 1).reshape(16, LANES)

    matrix = staged(matrix)
    values, columns = partial_value(place, piece, matrix)
    values = pair_summed(swapped(values.reshape(2, 16, WIDTH, LANES), "core"))
    values, lines = lax.optimization_barrier((values, lines))
    values = swapped(values, PLANE).sum(axis=0)
    far = shared(jnp.concatenate([values, lines], axis=0), "zh")
    summed = far[:, :WIDTH].sum(axis=0)
    own = jnp.concatenate([summed, far[:, WIDTH:].reshape(WIDTH, LANES)], axis=0)
    own = shared(shared(own, "zl"), "x")
    other = local(lax.ppermute(own, "core", [(0, 1), (1, 0)]))
    own = local(own)

    parts = local(swapped(left_parts(place, own, other, matrix), "row"))
    return last_step(place, parts, columns, own, other, matrix)


def solution(mesh):
    torus = Mesh(mesh.devices.reshape(4, 4, 4, 4, 2), AXES)
    placed = (P("row", COLUMNS), P(None, ("row", "zh", "zl")))
    return jax.shard_map(
        on_device, mesh=torus, in_specs=placed, out_specs=P("row", COLUMNS), check_vma=False
    )
```

```python
import jax
import jax.numpy as jnp
from jax import lax
from jax.experimental import pallas as pl
from jax.experimental.pallas import tpu as pltpu
from jax.sharding import Mesh
from jax.sharding import PartitionSpec as P

AXES = ("row", "zh", "zl", "x", "core")
COLUMNS = ("zh", "zl", "x", "core")
PLANE = ("zl", "x")
LANES = 128
WIDTH = 64
ROOM = pltpu.CompilerParams(vmem_limit_bytes=16 * 1024 * 1024)

highest = lax.Precision.HIGHEST
NN = ((1,), (0,))
NT = ((1,), (1,))
TN = ((0,), (0,))


def exact(left, right, dims):
    return lax.dot_general(
        left, right, (dims, ((), ())), precision=highest, preferred_element_type=jnp.float32
    )


def split(array):
    high = array.astype(jnp.bfloat16)
    return high, (array - high.astype(jnp.float32)).astype(jnp.bfloat16)


def dot(left, right, dims):
    return lax.dot_general(left, right, (dims, ((), ())), preferred_element_type=jnp.float32)


def swapped(array, axes):
    return lax.all_to_all(array, axes, 0, 0, tiled=True)


def shared(array, axes):
    return swapped(jnp.broadcast_to(array, (lax.axis_size(axes), *array.shape)), axes)


def mask_vectors(values, first_row):
    panel_width, row_count = values.shape
    positions = first_row + lax.iota(jnp.int32, row_count)[None, :]
    reflector = lax.iota(jnp.int32, panel_width)[:, None]
    filler = jnp.where(positions == reflector + 1, 1.0, 0.0).astype(values.dtype)
    return jnp.where(positions > reflector + 1, values, filler)


def column_routes():
    turn = {0: 2, 1: 1, 2: 0, 3: 3}
    pairs = []
    for y in range(4):
        for z in range(16):
            for x in range(4):
                for core in range(2):
                    to_x, to_z = z % 4, y * 4 + z // 4
                    to_y = (y + turn[(x - to_x) % 4]) % 4
                    here = ((y * 16 + z) * 4 + x) * 2 + core
                    pairs.append((here, ((to_y * 16 + to_z) * 4 + to_x) * 2 + core))
    return pairs


def doubled(array):
    blank = jnp.zeros_like(array)
    return jnp.concatenate(
        [jnp.concatenate([array, blank], axis=1), jnp.concatenate([blank, array], axis=1)], axis=0
    )


def local(array):
    return pltpu.with_memory_space_constraint(array, pltpu.VMEM)


def in_vmem(count):
    return [pl.BlockSpec(memory_space=pltpu.VMEM)] * count


def staging_kernel(matrix_ref, out_ref, sem):
    copy = pltpu.make_async_copy(matrix_ref, out_ref, sem)
    copy.start()
    copy.wait()


def staged(matrix):
    return pl.pallas_call(
        staging_kernel,
        in_specs=[pl.BlockSpec(memory_space=pltpu.HBM)],
        out_specs=in_vmem(1)[0],
        out_shape=pltpu.VMEM(matrix.shape, jnp.float32),
        scratch_shapes=[pltpu.SemaphoreType.DMA],
        compiler_params=ROOM,
        name="staging",
    )(pltpu.with_memory_space_constraint(matrix, pltpu.HBM))


def pair_kernel(pair_ref, out_ref):
    out_ref[...] = pair_ref[0] + pair_ref[1]


def pair_summed(pair):
    return pl.pallas_call(
        pair_kernel,
        in_specs=in_vmem(1),
        out_specs=in_vmem(1)[0],
        out_shape=pltpu.VMEM(pair.shape[1:], jnp.float32),
        compiler_params=ROOM,
        name="pair",
    )(local(pair))


def value_kernel(columns_ref, matrix_ref, out_ref):
    high, low = split(doubled(columns_ref[...].T))
    right = jnp.concatenate([high, low], axis=1)
    for unit in range(16):
        first = matrix_ref[2 * unit * LANES : (2 * unit + 1) * LANES, :]
        second = matrix_ref[(2 * unit + 1) * LANES : (2 * unit + 2) * LANES, :]
        high, low = split(jnp.concatenate([first, second], axis=1))
        both = dot(high, right, NN) + dot(low, right, NN)
        total = both[:, :LANES] + both[:, LANES:]
        out_ref[2 * unit : 2 * unit + 2] = total.reshape(2, WIDTH, LANES)


def partial_value(columns, matrix):
    return pl.pallas_call(
        value_kernel,
        in_specs=in_vmem(2),
        out_specs=in_vmem(1)[0],
        out_shape=pltpu.VMEM((32, WIDTH, LANES), jnp.float32),
        compiler_params=ROOM,
        name="value",
    )(columns, matrix)


def reflector_block(flag_ref, own_ref, other_ref, unit, half):
    zh, zl = divmod(unit, 4)
    start = WIDTH + zh * 16 + half * 8
    own, other = own_ref[:, zl, start : start + 8, :], other_ref[:, zl, start : start + 8, :]
    first = flag_ref[...] == 0
    rows = [jnp.where(first, own, other), jnp.where(first, other, own)]
    return jnp.concatenate(rows, axis=0).reshape(WIDTH, LANES)


def value_unit(flag_ref, own_ref, other_ref, unit):
    core, zl, x = unit // 8, unit // 2 % 4, 2 * unit % 4
    own, other = own_ref[x : x + 2, zl, :WIDTH, :], other_ref[x : x + 2, zl, :WIDTH, :]
    own, other = own.reshape(16, 8, LANES), other.reshape(16, 8, LANES)
    return jnp.where(flag_ref[...] == core, own, other).reshape(2 * WIDTH, LANES)


def in_three(array):
    high, low = split(array)
    rest = array - high.astype(jnp.float32) - low.astype(jnp.float32)
    return jnp.concatenate([high, low, rest.astype(jnp.bfloat16)], axis=0)


def terms_kernel(flag_ref, own_ref, other_ref, matrix_ref, out_ref):
    held = (flag_ref, own_ref, other_ref)
    plain = jnp.zeros((2 * WIDTH, 2 * LANES), jnp.float32)
    cross = jnp.zeros((4 * WIDTH, 2 * LANES), jnp.float32)
    gram = jnp.zeros((3 * WIDTH, 3 * WIDTH), jnp.float32)
    for unit in range(16):
        rows = [reflector_block(*held, unit, half) for half in range(2)]
        rows = in_three(jnp.concatenate(rows, axis=1))
        span = slice(2 * unit * LANES, 2 * (unit + 1) * LANES)
        right = jnp.concatenate(split(matrix_ref[span, :]), axis=1)
        plain += dot(rows[: 2 * WIDTH], right, NN)
        right = jnp.concatenate(split(value_unit(*held, unit)), axis=1)
        both = [rows[: 2 * WIDTH, :LANES], rows[: 2 * WIDTH, LANES:]]
        cross += dot(jnp.concatenate(both, axis=0), right, NN)
        gram += dot(rows, rows, NT)
    plain = plain[:WIDTH] + plain[WIDTH:]
    plain = plain[:, :LANES] + plain[:, LANES:]
    cross = cross[:, :LANES] + cross[:, LANES:]
    first = cross[:WIDTH] + cross[WIDTH : 2 * WIDTH]
    second = cross[2 * WIDTH : 3 * WIDTH] + cross[3 * WIDTH :]
    cross = first[:, :WIDTH] + second[:, WIDTH:]
    gram = gram[:WIDTH] + (gram[WIDTH : 2 * WIDTH] + gram[2 * WIDTH :])
    gram = gram[:, :WIDTH] + (gram[:, WIDTH : 2 * WIDTH] + gram[:, 2 * WIDTH :])
    joined = jnp.concatenate([plain, cross, gram], axis=1)
    for y in range(4):
        out_ref[y] = joined


def left_parts(held, matrix):
    return pl.pallas_call(
        terms_kernel,
        in_specs=in_vmem(4),
        out_specs=in_vmem(1)[0],
        out_shape=pltpu.VMEM((4, WIDTH, 2 * LANES), jnp.float32),
        compiler_params=ROOM,
        name="terms",
    )(*held, matrix)


def make_factor(gram):
    size_b = gram.shape[0]
    down = lax.broadcasted_iota(jnp.int32, (size_b, size_b), 0)
    across = lax.broadcasted_iota(jnp.int32, (size_b, size_b), 1)
    identity = jnp.where(down == across, 1.0, 0.0)
    half = 0.5 * jnp.where(down == across, gram, 0.0)
    half_down = jnp.sum(half, axis=1, keepdims=True)
    half_across = jnp.sum(half, axis=0, keepdims=True)
    scaled = jnp.where(across > down, gram, 0.0) / half_down
    inverse = identity - scaled
    powered = scaled
    for level in range((size_b - 1).bit_length() - 1):
        powered = exact(powered, powered, NN)
        inverse = exact(inverse, identity + powered, NN)
    return inverse / half_across


def last_kernel(
    parts_ref, columns_ref, flag_ref, own_ref, other_ref, matrix_ref, out_ref, done_ref, sems
):
    held = (flag_ref, own_ref, other_ref)
    total = (parts_ref[0] + parts_ref[1]) + (parts_ref[2] + parts_ref[3])
    factor = make_factor(total[:, LANES + WIDTH :])
    right = exact(factor, columns_ref[...], NN)
    left = total[:, :LANES] - exact(total[:, LANES : LANES + WIDTH], right, NN)
    left = exact(factor, left, TN)
    high, low = split(jnp.concatenate([doubled(right), doubled(left)], axis=0))
    copies = []
    for unit in range(16):
        rows = [reflector_block(*held, unit, half) for half in range(2)]
        rows = jnp.concatenate(rows, axis=0).T
        left = split(jnp.concatenate([value_unit(*held, unit), rows], axis=1))
        change = dot(left[0], high, NN) + (dot(left[0], low, NN) + dot(left[1], high, NN))
        for half in range(2):
            start = (2 * unit + half) * LANES
            span = slice(start, start + LANES)
            done_ref[span, :] = matrix_ref[span, :] - change[:, half * LANES : (half + 1) * LANES]
        if unit % 4 == 3:
            part = pl.ds((unit - 3) * 2 * LANES, 8 * LANES)
            copy = pltpu.make_async_copy(done_ref.at[part], out_ref.at[part], sems.at[unit // 4])
            copy.start()
            copies.append(copy)
    for copy in copies:
        copy.wait()


def last_step(parts, columns, held, matrix):
    return pl.pallas_call(
        last_kernel,
        in_specs=in_vmem(6),
        out_specs=pl.BlockSpec(memory_space=pl.ANY),
        out_shape=jax.ShapeDtypeStruct(matrix.shape, jnp.float32),
        scratch_shapes=[
            pltpu.VMEM(matrix.shape, jnp.float32),
            pltpu.SemaphoreType.DMA((4,)),
        ],
        compiler_params=ROOM,
        name="last",
    )(parts, columns, *held, matrix)


def on_device(matrix, vectors):
    width, piece = vectors.shape
    core, x = lax.axis_index("core"), lax.axis_index("x")
    masked = mask_vectors(vectors, lax.axis_index(("row", "zh", "zl")) * piece)
    half = lax.dynamic_slice_in_dim(masked, core * LANES, LANES, 1)
    columns = lax.ppermute(half, AXES, column_routes())
    lines = lax.dynamic_slice_in_dim(masked, (core * 4 + x) * 8, 8, 0)
    lines = lines.reshape(8, 2, LANES).swapaxes(0, 1).reshape(16, LANES)

    matrix, columns = staged(matrix), local(columns)
    values = partial_value(columns, matrix)
    values = pair_summed(swapped(values.reshape(2, 16, WIDTH, LANES), "core"))
    flag = jnp.full((8, LANES), core, jnp.int32)
    values, lines, flag = lax.optimization_barrier((values, lines, flag))
    values = swapped(values, PLANE).sum(axis=0)
    far = shared(jnp.concatenate([values, lines], axis=0), "zh")
    summed = far[:, :WIDTH].sum(axis=0)
    own = jnp.concatenate([summed, far[:, WIDTH:].reshape(WIDTH, LANES)], axis=0)
    own = shared(shared(own, "zl"), "x")
    other = lax.ppermute(own, "core", [(0, 1), (1, 0)])
    held = (local(flag), local(own), local(other))

    parts = local(swapped(left_parts(held, matrix), "row"))
    return last_step(parts, columns, held, matrix)


def solution(mesh):
    torus = Mesh(mesh.devices.reshape(4, 4, 4, 4, 2), AXES)
    placed = (P("row", COLUMNS), P(None, ("row", "zh", "zl")))
    return jax.shard_map(
        on_device, mesh=torus, in_specs=placed, out_specs=P("row", COLUMNS), check_vma=False
    )
```

```python
import jax
import jax.numpy as jnp
from jax import lax
from jax.experimental import pallas as pl
from jax.experimental.pallas import tpu as pltpu
from jax.sharding import Mesh
from jax.sharding import PartitionSpec as P

AXES = ("row", "zh", "zl", "x", "core")
COLUMNS = ("zh", "zl", "x", "core")
PLANE = ("zl", "x")
LANES = 128
WIDTH = 64
ROOM = pltpu.CompilerParams(vmem_limit_bytes=16 * 1024 * 1024)

highest = lax.Precision.HIGHEST
NN = ((1,), (0,))
NT = ((1,), (1,))
TN = ((0,), (0,))


def exact(left, right, dims):
    return lax.dot_general(
        left, right, (dims, ((), ())), precision=highest, preferred_element_type=jnp.float32
    )


def split(array):
    high = array.astype(jnp.bfloat16)
    return high, (array - high.astype(jnp.float32)).astype(jnp.bfloat16)


def dot(left, right, dims):
    return lax.dot_general(left, right, (dims, ((), ())), preferred_element_type=jnp.float32)


def swapped(array, axes):
    return lax.all_to_all(array, axes, 0, 0, tiled=True)


def shared(array, axes):
    return swapped(jnp.broadcast_to(array, (lax.axis_size(axes), *array.shape)), axes)


def mask_vectors(values, first_row):
    panel_width, row_count = values.shape
    positions = first_row + lax.iota(jnp.int32, row_count)[None, :]
    reflector = lax.iota(jnp.int32, panel_width)[:, None]
    filler = jnp.where(positions == reflector + 1, 1.0, 0.0).astype(values.dtype)
    return jnp.where(positions > reflector + 1, values, filler)


def column_routes():
    turn = {0: 2, 1: 1, 2: 0, 3: 3}
    pairs = []
    for y in range(4):
        for z in range(16):
            for x in range(4):
                for core in range(2):
                    to_x, to_z = z % 4, y * 4 + z // 4
                    to_y = (y + turn[(x - to_x) % 4]) % 4
                    here = ((y * 16 + z) * 4 + x) * 2 + core
                    pairs.append((here, ((to_y * 16 + to_z) * 4 + to_x) * 2 + core))
    return pairs


def doubled(array):
    blank = jnp.zeros_like(array)
    return jnp.concatenate(
        [jnp.concatenate([array, blank], axis=1), jnp.concatenate([blank, array], axis=1)], axis=0
    )


def local(array):
    return pltpu.with_memory_space_constraint(array, pltpu.VMEM)


def in_vmem(count):
    return [pl.BlockSpec(memory_space=pltpu.VMEM)] * count


def staging_kernel(matrix_ref, out_ref, sem):
    copy = pltpu.make_async_copy(matrix_ref, out_ref, sem)
    copy.start()
    copy.wait()


def staged(matrix):
    return pl.pallas_call(
        staging_kernel,
        in_specs=[pl.BlockSpec(memory_space=pltpu.HBM)],
        out_specs=in_vmem(1)[0],
        out_shape=pltpu.VMEM(matrix.shape, jnp.float32),
        scratch_shapes=[pltpu.SemaphoreType.DMA],
        compiler_params=ROOM,
        name="staging",
    )(pltpu.with_memory_space_constraint(matrix, pltpu.HBM))


def pair_kernel(kept_ref, sent_ref, out_ref):
    out_ref[...] = kept_ref[...] + sent_ref[...]


def pair_summed(kept, sent):
    return pl.pallas_call(
        pair_kernel,
        in_specs=in_vmem(2),
        out_specs=in_vmem(1)[0],
        out_shape=pltpu.VMEM(kept.shape, jnp.float32),
        compiler_params=ROOM,
        name="pair",
    )(kept, local(sent))


def value_kernel(flag_ref, columns_ref, matrix_ref, keep_ref, send_ref):
    high, low = split(doubled(columns_ref[...].T))
    right = jnp.concatenate([high, low], axis=1)
    first = flag_ref[...] == 0
    for unit in range(8):
        low, high = [value_rows(matrix_ref, right, k) for k in (unit, unit + 8)]
        span = slice(2 * unit, 2 * unit + 2)
        keep_ref[span] = jnp.where(first, low, high).reshape(2, WIDTH, LANES)
        send_ref[span] = jnp.where(first, high, low).reshape(2, WIDTH, LANES)


def value_rows(matrix_ref, right, unit):
    first = matrix_ref[2 * unit * LANES : (2 * unit + 1) * LANES, :]
    second = matrix_ref[(2 * unit + 1) * LANES : (2 * unit + 2) * LANES, :]
    high, low = split(jnp.concatenate([first, second], axis=1))
    both = dot(high, right, NN) + dot(low, right, NN)
    return (both[:, :LANES] + both[:, LANES:]).reshape(16, 8, LANES)


def partial_value(flag, columns, matrix):
    return pl.pallas_call(
        value_kernel,
        in_specs=in_vmem(3),
        out_specs=in_vmem(2),
        out_shape=[pltpu.VMEM((16, WIDTH, LANES), jnp.float32)] * 2,
        compiler_params=ROOM,
        name="value",
    )(flag, columns, matrix)


def reflector_block(flag_ref, own_ref, other_ref, unit, half):
    zh, zl = divmod(unit, 4)
    start = WIDTH + zh * 16 + half * 8
    own, other = own_ref[:, zl, start : start + 8, :], other_ref[:, zl, start : start + 8, :]
    first = flag_ref[...] == 0
    rows = [jnp.where(first, own, other), jnp.where(first, other, own)]
    return jnp.concatenate(rows, axis=0).reshape(WIDTH, LANES)


def value_unit(flag_ref, own_ref, other_ref, unit):
    core, zl, x = unit // 8, unit // 2 % 4, 2 * unit % 4
    own, other = own_ref[x : x + 2, zl, :WIDTH, :], other_ref[x : x + 2, zl, :WIDTH, :]
    own, other = own.reshape(16, 8, LANES), other.reshape(16, 8, LANES)
    return jnp.where(flag_ref[...] == core, own, other).reshape(2 * WIDTH, LANES)


def in_three(array):
    high, low = split(array)
    rest = array - high.astype(jnp.float32) - low.astype(jnp.float32)
    return jnp.concatenate([high, low, rest.astype(jnp.bfloat16)], axis=0)


def terms_kernel(flag_ref, own_ref, other_ref, matrix_ref, out_ref):
    held = (flag_ref, own_ref, other_ref)
    plain = jnp.zeros((2 * WIDTH, 2 * LANES), jnp.float32)
    cross = jnp.zeros((4 * WIDTH, 2 * LANES), jnp.float32)
    gram = jnp.zeros((3 * WIDTH, 3 * WIDTH), jnp.float32)
    for unit in range(16):
        rows = [reflector_block(*held, unit, half) for half in range(2)]
        rows = in_three(jnp.concatenate(rows, axis=1))
        span = slice(2 * unit * LANES, 2 * (unit + 1) * LANES)
        right = jnp.concatenate(split(matrix_ref[span, :]), axis=1)
        plain += dot(rows[: 2 * WIDTH], right, NN)
        right = jnp.concatenate(split(value_unit(*held, unit)), axis=1)
        both = [rows[: 2 * WIDTH, :LANES], rows[: 2 * WIDTH, LANES:]]
        cross += dot(jnp.concatenate(both, axis=0), right, NN)
        gram += dot(rows, rows, NT)
    plain = plain[:WIDTH] + plain[WIDTH:]
    plain = plain[:, :LANES] + plain[:, LANES:]
    cross = cross[:, :LANES] + cross[:, LANES:]
    first = cross[:WIDTH] + cross[WIDTH : 2 * WIDTH]
    second = cross[2 * WIDTH : 3 * WIDTH] + cross[3 * WIDTH :]
    cross = first[:, :WIDTH] + second[:, WIDTH:]
    gram = gram[:WIDTH] + (gram[WIDTH : 2 * WIDTH] + gram[2 * WIDTH :])
    gram = gram[:, :WIDTH] + (gram[:, WIDTH : 2 * WIDTH] + gram[:, 2 * WIDTH :])
    joined = jnp.concatenate([plain, cross, gram], axis=1)
    for y in range(4):
        out_ref[y] = joined


def left_parts(held, matrix):
    return pl.pallas_call(
        terms_kernel,
        in_specs=in_vmem(4),
        out_specs=in_vmem(1)[0],
        out_shape=pltpu.VMEM((4, WIDTH, 2 * LANES), jnp.float32),
        compiler_params=ROOM,
        name="terms",
    )(*held, matrix)


def make_factor(gram):
    size_b = gram.shape[0]
    down = lax.broadcasted_iota(jnp.int32, (size_b, size_b), 0)
    across = lax.broadcasted_iota(jnp.int32, (size_b, size_b), 1)
    identity = jnp.where(down == across, 1.0, 0.0)
    half = 0.5 * jnp.where(down == across, gram, 0.0)
    half_down = jnp.sum(half, axis=1, keepdims=True)
    half_across = jnp.sum(half, axis=0, keepdims=True)
    scaled = jnp.where(across > down, gram, 0.0) / half_down
    inverse = identity - scaled
    powered = scaled
    for level in range((size_b - 1).bit_length() - 1):
        powered = exact(powered, powered, NN)
        inverse = exact(inverse, identity + powered, NN)
    return inverse / half_across


def last_kernel(
    parts_ref, columns_ref, flag_ref, own_ref, other_ref, matrix_ref, out_ref, done_ref, sems
):
    held = (flag_ref, own_ref, other_ref)
    total = (parts_ref[0] + parts_ref[1]) + (parts_ref[2] + parts_ref[3])
    factor = make_factor(total[:, LANES + WIDTH :])
    right = exact(factor, columns_ref[...], NN)
    left = total[:, :LANES] - exact(total[:, LANES : LANES + WIDTH], right, NN)
    left = exact(factor, left, TN)
    high, low = split(jnp.concatenate([doubled(right), doubled(left)], axis=0))
    copies = []
    for unit in range(16):
        rows = [reflector_block(*held, unit, half) for half in range(2)]
        rows = jnp.concatenate(rows, axis=0).T
        left = split(jnp.concatenate([value_unit(*held, unit), rows], axis=1))
        change = dot(left[0], high, NN) + (dot(left[0], low, NN) + dot(left[1], high, NN))
        for half in range(2):
            start = (2 * unit + half) * LANES
            span = slice(start, start + LANES)
            done_ref[span, :] = matrix_ref[span, :] - change[:, half * LANES : (half + 1) * LANES]
        if unit % 4 == 3:
            part = pl.ds((unit - 3) * 2 * LANES, 8 * LANES)
            copy = pltpu.make_async_copy(done_ref.at[part], out_ref.at[part], sems.at[unit // 4])
            copy.start()
            copies.append(copy)
    for copy in copies:
        copy.wait()


def last_step(parts, columns, held, matrix):
    return pl.pallas_call(
        last_kernel,
        in_specs=in_vmem(6),
        out_specs=pl.BlockSpec(memory_space=pl.ANY),
        out_shape=jax.ShapeDtypeStruct(matrix.shape, jnp.float32),
        scratch_shapes=[
            pltpu.VMEM(matrix.shape, jnp.float32),
            pltpu.SemaphoreType.DMA((4,)),
        ],
        compiler_params=ROOM,
        name="last",
    )(parts, columns, *held, matrix)


def on_device(matrix, vectors):
    width, piece = vectors.shape
    core, x = lax.axis_index("core"), lax.axis_index("x")
    masked = mask_vectors(vectors, lax.axis_index(("row", "zh", "zl")) * piece)
    half = lax.dynamic_slice_in_dim(masked, core * LANES, LANES, 1)
    columns = lax.ppermute(half, AXES, column_routes())
    lines = lax.dynamic_slice_in_dim(masked, (core * 4 + x) * 8, 8, 0)
    lines = lines.reshape(8, 2, LANES).swapaxes(0, 1).reshape(16, LANES)

    matrix, columns = staged(matrix), local(columns)
    flag = jnp.full((8, LANES), core, jnp.int32)
    kept, sent = partial_value(local(flag), columns, matrix)
    values = pair_summed(kept, lax.ppermute(local(sent), "core", [(0, 1), (1, 0)]))
    values, lines, flag = lax.optimization_barrier((values, lines, flag))
    values = swapped(values, PLANE).sum(axis=0)
    far = shared(jnp.concatenate([values, lines], axis=0), "zh")
    summed = far[:, :WIDTH].sum(axis=0)
    own = jnp.concatenate([summed, far[:, WIDTH:].reshape(WIDTH, LANES)], axis=0)
    own = shared(shared(own, "zl"), "x")
    other = lax.ppermute(own, "core", [(0, 1), (1, 0)])
    held = (local(flag), local(own), local(other))

    parts = local(swapped(left_parts(held, matrix), "row"))
    return last_step(parts, columns, held, matrix)


def solution(mesh):
    torus = Mesh(mesh.devices.reshape(4, 4, 4, 4, 2), AXES)
    placed = (P("row", COLUMNS), P(None, ("row", "zh", "zl")))
    return jax.shard_map(
        on_device, mesh=torus, in_specs=placed, out_specs=P("row", COLUMNS), check_vma=False
    )
```
